512 devices in a mesh: gx: 32 (over y, x), gy: 16 (over z, core).
Axes of the slice: x: 4, y: 8, z: 8, core: 2. Of those that a mesh axis runs over, the one named last changes fastest.
Arguments:
- hidden_in: bfloat16 [4096, 2560], P('gx'), may hold values from -48 to 48
- norm_gain: bfloat16 [2560], replicated, may hold values from 0.099609375 to 1.8984375
- router_weight: bfloat16 [2560, 64], replicated, may hold values from -3 to 3
- routes: int32 [4096, 6], P('gx'), may hold values from 0 to 63, as said below
- w_gate_up: bfloat16 [512, 2560, 384], P(('gx', 'gy')), may hold values from -0.125 to 0.125
- w_down: bfloat16 [512, 192, 2560], P(('gx', 'gy')), may hold values from -0.15625 to 0.15625
- final_gain: bfloat16 [2560], replicated, may hold values from 0.099609375 to 1.8984375
- head_weight: bfloat16 [2560, 53248], P('gy', 'gx'), may hold values from -5 to 5
- targets: int32 [4096], replicated, may hold values from 0 to 53247
Outputs:
- logprob: float32 [32, 128], P(None, 'gy')
- entropy: float32 [32, 128], P(None, 'gy')
The draws below stay inside these ranges and needn't reach their ends.
Inputs may be any that keep to these rules, and one draw needn't show every extreme that they name: `routes`: each row names 6 different experts. Within the 128 rows of one index of gx no expert is named by more than 16 rows, and one expert, the same for every index of gx, is named by exactly 16 rows in each.
All inputs are finite; a program needn't handle non-finite values.
Results may differ from the reference program's by a relative error of at most 0.012.
Values may be sent and summed in bfloat16 or wider, within the bound.
A program may use at most 192 MiB of HBM per device.

```python
import math
import jax
import jax.numpy as jnp
from jax import lax

D = 2560
E = 64
TOPK = 6
FF = 1536
V = 53248
SPLITS = 8
TOK_DEV = 128
TOKENS = 4096
CAP = 16
FP = 192
N_GX = 32


def draw_hidden_in(key, part):
    own_key = jax.random.fold_in(key, 11)
    key_noise, key_rows, key_cols = jax.random.split(own_key, 3)
    row_scale = jnp.exp(jax.random.uniform(key_rows, (TOKENS, 1), minval=math.log(0.25), maxval=math.log(2.5)))
    col_scale = jnp.exp(jax.random.uniform(key_cols, (1, D), minval=math.log(0.3), maxval=math.log(3.0)))
    noise = jnp.clip(jax.random.normal(key_noise, (TOKENS, D)), -6.0, 6.0)
    values = noise * row_scale * col_scale
    return values.astype(jnp.bfloat16)


def draw_router_weight(key, part):
    own_key = jax.random.fold_in(key, 13)
    key_noise = jax.random.fold_in(own_key, 0)
    values = jnp.clip(jax.random.normal(key_noise, (D, E)), -4.0, 4.0) * (1.0 / math.sqrt(D))
    return values.astype(jnp.bfloat16)


def draw_head_weight(key, part):
    own_key = jax.random.fold_in(key, 17)
    key_noise, key_scale = jax.random.split(own_key, 2)
    col_scale = jnp.exp(jax.random.uniform(key_scale, (1, V), minval=0.0, maxval=math.log(10.0))) * (0.7 / math.sqrt(D))
    noise = jnp.clip(jax.random.normal(key_noise, (D, V)), -4.0, 4.0)
    values = noise * col_scale
    return values.astype(jnp.bfloat16)


def draw_routes(key, part):
    blocks = TOKENS // TOK_DEV
    base_load = TOK_DEV * TOPK // E
    headroom = CAP - base_load
    pairing = jax.random.permutation(jax.random.fold_in(key, 101), E)

    def one_block(block_index):
        block_key = jax.random.fold_in(jax.random.fold_in(key, 202), block_index)
        key_shift, key_list, key_rows, key_order = jax.random.split(block_key, 4)
        shifts = jax.random.randint(key_shift, (E // 2,), 0, headroom + 1)
        shifts = shifts.at[0].set(headroom)
        paired = jnp.stack([base_load + shifts, base_load - shifts], axis=1).reshape(E)
        expert_loads = jnp.zeros((E,), jnp.int32).at[pairing].set(paired)
        listing = jax.random.permutation(key_list, E)
        bounds = jnp.cumsum(expert_loads[listing])
        position = jnp.arange(TOK_DEV * TOPK)
        rank_list = jnp.sum((bounds[None, :] <= position[:, None]).astype(jnp.int32), axis=1)
        flat_list = listing[rank_list]
        route_grid = flat_list.reshape(TOPK, TOK_DEV).T
        route_grid = route_grid[jax.random.permutation(key_rows, TOK_DEV)]
        slot_keys = jax.random.randint(key_order, (TOK_DEV, TOPK), 0, 1048576) * TOPK + jnp.arange(TOPK)[None, :]
        slot_order = jnp.argsort(slot_keys, axis=1, stable=True)
        return jnp.take_along_axis(route_grid, slot_order, axis=1)
    return jax.vmap(one_block)(jnp.arange(blocks)).reshape(TOKENS, TOPK).astype(jnp.int32)


def plant(result, key, least, largest):
    place = [jax.random.randint(jax.random.fold_in(key, axis), (), 0, length) for axis, length in enumerate(result.shape)]
    main_axis = result.shape.index(max(result.shape))
    beside = place[:main_axis] + [(place[main_axis] + 1) % result.shape[main_axis]] + place[main_axis + 1:]
    return result.at[tuple(place)].set(least).at[tuple(beside)].set(largest)


def shard_levels(key, dims, cuts, smallest, high):
    loudness, own = 1.0, jax.random.fold_in(key, 6)
    for axis_at, parts in cuts:
        draws = jnp.exp(jax.random.uniform(jax.random.fold_in(own, axis_at), (parts,), jnp.float32, smallest / len(cuts), high / len(cuts)))
        loudness = loudness * jnp.repeat(draws, dims[axis_at] // parts).reshape([-1 if axis == axis_at else 1 for axis in range(len(dims))])
    return loudness


def normal_values(rng, extent, scale, limit, pieces=(), held_as=jnp.bfloat16):
    factor_of = shard_levels(rng, extent, pieces, -0.22, 0.18) if pieces else 1.0
    array = jax.random.normal(rng, extent, jnp.float32) * scale * factor_of
    return jnp.minimum(jnp.maximum(array, -limit), limit).astype(held_as)


def setup_inputs(seed: int = 0) -> dict:
    key_of = jax.random.split(jax.random.key(seed), 10)
    return {
        "hidden_in": draw_hidden_in(jax.random.fold_in(key_of[9], 71), 0),
        "norm_gain": jnp.clip(1.0 + 0.18 * jax.random.normal(key_of[1], (D,), jnp.float32), 0.099609375, 1.8984375).astype(jnp.bfloat16),
        "router_weight": draw_router_weight(jax.random.fold_in(key_of[9], 71), 0),
        "routes": draw_routes(jax.random.fold_in(key_of[9], 71), 0),
        "w_gate_up": normal_values(key_of[4], (E * SPLITS, D, 2 * FP), D ** -0.5, 0.125, ((0, 512),)),
        "w_down": normal_values(key_of[5], (E * SPLITS, FP, D), FF ** -0.5, 0.15625, ((0, 512),)),
        "final_gain": jnp.clip(1.0 + 0.18 * jax.random.normal(key_of[6], (D,), jnp.float32), 0.099609375, 1.8984375).astype(jnp.bfloat16),
        "head_weight": draw_head_weight(jax.random.fold_in(key_of[9], 71), 0),
        "targets": plant(jax.random.randint(key_of[8], (TOKENS,), 0, V), jax.random.fold_in(key_of[8], 1), 0, V - 1).astype(jnp.int32),
    }


NORM_EPSILON = 1e-06

def rms_scale(values, gain_vector):
    widened = values.astype(jnp.float32)
    return widened * lax.rsqrt(lax.optimization_barrier(jnp.mean(widened * widened, -1, keepdims=True)) + NORM_EPSILON) * gain_vector.astype(jnp.float32)

def reference(hidden_in, norm_gain, router_weight, routes, w_gate_up, w_down, final_gain, head_weight, targets):
    normed = rms_scale(hidden_in, norm_gain).astype(jnp.bfloat16)
    scores = jnp.dot(normed, router_weight, preferred_element_type=jnp.float32)
    picked = jnp.take_along_axis(scores, routes, axis=1)
    gate_values = lax.optimization_barrier(jax.nn.softmax(picked, axis=-1).astype(jnp.bfloat16)).astype(jnp.float32)
    unit_count = w_down.shape[1]
    most_rows = N_GX * CAP
    normed_wide = normed.astype(jnp.float32)

    def expert_step(routed, expert_id):
        member = routes == expert_id
        weight_row = lax.optimization_barrier(jnp.sum(jnp.where(member, gate_values, 0.0), -1))
        taken = jnp.any(member, -1)
        positions = jnp.nonzero(taken, size=most_rows, fill_value=0)[0].astype(jnp.int32)
        live_rows = (jnp.arange(most_rows) < jnp.sum(taken.astype(jnp.int32))).astype(jnp.float32)
        expert_rows = normed_wide[positions]
        first_slice = expert_id * SPLITS
        gate_up = lax.dynamic_slice_in_dim(w_gate_up, first_slice, SPLITS, 0).astype(jnp.float32)
        down_proj = lax.dynamic_slice_in_dim(w_down, first_slice, SPLITS, 0).astype(jnp.float32)
        lifted = jnp.einsum('nd,pdf->pnf', expert_rows, gate_up)
        active = jax.nn.silu(lifted[..., :unit_count]) * lifted[..., unit_count:]
        active = lax.optimization_barrier(active.astype(jnp.bfloat16)).astype(jnp.float32)
        part_out = jnp.einsum('pnf,pfd->pnd', active, down_proj)
        part_out = lax.optimization_barrier(part_out.astype(jnp.bfloat16)).astype(jnp.float32)
        merged = lax.optimization_barrier(jnp.sum(part_out, 0)) * (weight_row[positions] * live_rows)[:, None]
        return (routed.at[positions].add(merged), None)
    routed, ignored_out = lax.scan(expert_step, jnp.zeros(hidden_in.shape, jnp.float32), jnp.arange(E, dtype=jnp.int32))
    layer_out = lax.optimization_barrier((hidden_in.astype(jnp.float32) + routed).astype(jnp.bfloat16))
    final_states = lax.optimization_barrier(rms_scale(layer_out, final_gain).astype(jnp.bfloat16))
    head_wide = head_weight.astype(jnp.float32)

    def score_group(packed):
        group_states, group_targets = packed
        logits = jnp.dot(group_states.astype(jnp.float32), head_wide, preferred_element_type=jnp.float32)
        peak_value = lax.optimization_barrier(jnp.max(logits, -1, keepdims=True))
        shifted = logits - peak_value
        weights = jnp.exp(shifted)
        total_mass = lax.optimization_barrier(jnp.sum(weights, -1))
        spread = lax.optimization_barrier(jnp.sum(weights * shifted, -1))
        target_logit = jnp.take_along_axis(logits, group_targets[:, None], axis=1)[:, 0]
        return (target_logit - peak_value[:, 0] - jnp.log(total_mass), jnp.log(total_mass) - spread / total_mass)
    logprob, entropy = lax.map(score_group, (final_states.reshape(N_GX, TOK_DEV, D), targets.reshape(N_GX, TOK_DEV)))
    return (logprob, entropy)
```

```python
import functools

import jax
import jax.numpy as jnp
from jax import lax
from jax.experimental import pallas as pl
from jax.experimental.pallas import tpu as pltpu
from jax.sharding import PartitionSpec as P

SPLITS = 8
X_CHIPS = 4

NORM_EPSILON = 1e-06

VMEM = pl.BlockSpec(memory_space=pltpu.VMEM)
ANY = pl.BlockSpec(memory_space=pl.ANY)


def rms_scale(values, gain_vector):
    widened = values.astype(jnp.float32)
    return (
        widened
        * lax.rsqrt(jnp.mean(widened * widened, -1, keepdims=True) + NORM_EPSILON)
        * gain_vector.astype(jnp.float32)
    )


def remote(src, dst, send_sem, recv_sem, device):
    return pltpu.make_async_remote_copy(
        src_ref=src,
        dst_ref=dst,
        send_sem=send_sem,
        recv_sem=recv_sem,
        device_id=device,
        device_id_type=pl.DeviceIdType.MESH,
    )


def greet(devices):
    barrier = pltpu.get_barrier_semaphore()
    for device in devices:
        pl.semaphore_signal(
            barrier, inc=1, device_id=device, device_id_type=pl.DeviceIdType.MESH
        )
    pl.semaphore_wait(barrier, len(devices))


def offsets(axis, count):
    if axis == "gy":
        steps = [1]
        for z in range(1, count // 4 + 1):
            for sign in (1, -1):
                if sign == 1 or 2 * z != count // 2:
                    steps += [(sign * z, 0), (sign * z, 1)]
        return steps
    y_chips = count // X_CHIPS
    steps = []
    for y in range(0, y_chips // 2 + 1):
        for x in range(X_CHIPS):
            for sign in (1, -1):
                if (y == 0 or 2 * y == y_chips) and sign == -1:
                    continue
                if y or x:
                    steps.append((sign * y, x))
    return steps


def partners(axis, count, me):
    if axis == "gy":
        chips = count // 2
        z, core = me // 2, lax.rem(me, 2)
        found = [me + 1 - 2 * core]
        for step in offsets(axis, count)[1:]:
            found.append(
                lax.rem(z + step[0] + chips, chips) * 2 + lax.rem(core + step[1], 2)
            )
        return found
    y_chips = count // X_CHIPS
    y, x = me // X_CHIPS, lax.rem(me, X_CHIPS)
    return [
        lax.rem(y + dy + y_chips, y_chips) * X_CHIPS + lax.rem(x + dx, X_CHIPS)
        for dy, dx in offsets(axis, count)
    ]


def exchange_kernel(axis, same, count, *refs):
    src, out, send_sem, recv_sem, own_sem = refs
    me = lax.axis_index(axis)
    others = partners(axis, count, me)
    greet([{axis: other} for other in others])
    copies = [
        remote(
            src if same else src.at[other],
            out.at[me],
            send_sem.at[other],
            recv_sem.at[me],
            {axis: other},
        )
        for other in others
    ]
    for copy in copies:
        copy.start()
    own = pltpu.make_async_copy(src if same else src.at[me], out.at[me], own_sem)
    own.start()
    own.wait()
    for other in others:
        remote(
            src if same else src.at[other],
            out.at[other],
            send_sem.at[other],
            recv_sem.at[other],
            {axis: other},
        ).wait_recv()
    for copy in copies:
        copy.wait_send()


def exchange(values, axis, collective_id, same=False):
    count = lax.axis_size(axis)
    shape = (count,) + values.shape if same else values.shape
    return pl.pallas_call(
        functools.partial(exchange_kernel, axis, same, count),
        out_shape=jax.ShapeDtypeStruct(shape, values.dtype),
        in_specs=[VMEM],
        out_specs=VMEM,
        scratch_shapes=[
            pltpu.SemaphoreType.DMA((count,)),
            pltpu.SemaphoreType.DMA((count,)),
            pltpu.SemaphoreType.DMA,
        ],
        compiler_params=pltpu.CompilerParams(collective_id=collective_id, has_side_effects=True),
        cost_estimate=pl.CostEstimate(
            flops=0, bytes_accessed=40_000_000, transcendentals=0
        ),
    )(values)


def dispatch_kernel(count, *refs):
    (src, up, down, out, other_up, other_down, send_sem, recv_sem, own_sem, pair_sems) = refs
    me = lax.axis_index("gx")
    lane = lax.axis_index("gy")
    others = partners("gx", count, me)
    pair = {"gy": lane + 1 - 2 * lax.rem(lane, 2)}
    greet([pair] + [{"gx": other} for other in others])
    copies = [
        remote(
            src.at[other], out.at[me], send_sem.at[other], recv_sem.at[me], {"gx": other}
        )
        for other in others
    ]
    swaps = [
        remote(up, other_up, pair_sems.at[0], pair_sems.at[1], pair),
        remote(down, other_down, pair_sems.at[2], pair_sems.at[3], pair),
    ]
    for copy in copies:
        copy.start()
    for copy in swaps:
        copy.start()
    own = pltpu.make_async_copy(src.at[me], out.at[me], own_sem)
    own.start()
    own.wait()
    for other in others:
        remote(
            src.at[other], out.at[other], send_sem.at[other], recv_sem.at[other], {"gx": other}
        ).wait_recv()
    for copy in copies:
        copy.wait_send()
    for copy in swaps:
        copy.wait()


def dispatch_rows(values, up, down, collective_id):
    count = lax.axis_size("gx")
    return pl.pallas_call(
        functools.partial(dispatch_kernel, count),
        out_shape=(
            jax.ShapeDtypeStruct(values.shape, values.dtype),
            jax.ShapeDtypeStruct(up.shape, up.dtype),
            jax.ShapeDtypeStruct(down.shape, down.dtype),
        ),
        in_specs=[VMEM, ANY, ANY],
        out_specs=(VMEM, ANY, ANY),
        scratch_shapes=[
            pltpu.SemaphoreType.DMA((count,)),
            pltpu.SemaphoreType.DMA((count,)),
            pltpu.SemaphoreType.DMA,
            pltpu.SemaphoreType.DMA((4,)),
        ],
        compiler_params=pltpu.CompilerParams(collective_id=collective_id, has_side_effects=True),
        cost_estimate=pl.CostEstimate(
            flops=0, bytes_accessed=100_000_000, transcendentals=0
        ),
    )(values, up, down)


def relay_kernel(count, *refs):
    src, out, send_sem, recv_sem, own_sem = refs
    me = lax.axis_index("gx")
    y_chips = count // X_CHIPS
    y, x = me // X_CHIPS, lax.rem(me, X_CHIPS)

    def at(row, column):
        return lax.rem(row + y_chips, y_chips) * X_CHIPS + lax.rem(column, X_CHIPS)

    above, below = at(y + 1, x), at(y - 1, x)
    sides = [at(y, x + 1), at(y, x + 3), at(y, x + 2)]
    greet([{"gx": other} for other in [above, below] + sides])
    sent = []

    def send(block, source, target):
        copy = remote(
            source, out.at[block], send_sem.at[len(sent)], recv_sem.at[block], {"gx": target}
        )
        copy.start()
        sent.append(copy)

    def arrived(block):
        remote(
            src, out.at[block], send_sem.at[0], recv_sem.at[block], {"gx": above}
        ).wait_recv()

    send(me, src, above)
    send(me, src, below)
    for side in sides:
        send(me, src, side)
    own = pltpu.make_async_copy(src, out.at[me], own_sem)
    own.start()
    half = y_chips // 2
    for step in range(1, half + 1):
        block = at(y - step, x)
        arrived(block)
        if step < half:
            send(block, out.at[block], above)
        for side in sides:
            send(block, out.at[block], side)
        if step < half:
            block = at(y + step, x)
            arrived(block)
            if step < half - 1:
                send(block, out.at[block], below)
            for side in sides:
                send(block, out.at[block], side)
    for row in range(y_chips):
        for column in range(1, X_CHIPS):
            arrived(at(y + row, x + column))
    own.wait()
    for copy in sent:
        copy.wait_send()


def relay_gather(values, collective_id):
    count = lax.axis_size("gx")
    return pl.pallas_call(
        functools.partial(relay_kernel, count),
        out_shape=jax.ShapeDtypeStruct((count,) + values.shape, values.dtype),
        in_specs=[VMEM],
        out_specs=VMEM,
        scratch_shapes=[
            pltpu.SemaphoreType.DMA((count,)),
            pltpu.SemaphoreType.DMA((count,)),
            pltpu.SemaphoreType.DMA,
        ],
        compiler_params=pltpu.CompilerParams(collective_id=collective_id, has_side_effects=True),
        cost_estimate=pl.CostEstimate(
            flops=0, bytes_accessed=40_000_000, transcendentals=0
        ),
    )(values)


def shards(
    hidden_in, norm_gain, router_weight, routes, w_gate_up, w_down, final_gain, head_weight, targets
):
    tok_rows = hidden_in.shape[0]
    width = hidden_in.shape[1]
    group_count = lax.axis_size("gx")
    lane_count = lax.axis_size("gy")
    group_index = lax.axis_index("gx")
    lane_index = lax.axis_index("gy")
    expert_count = router_weight.shape[1]
    unit_count = w_down.shape[1]
    slot_count = tok_rows // 16
    share_rows = tok_rows // lane_count
    columns = head_weight.shape[1]
    head_full = lax.all_gather(head_weight, "gy", axis=0, tiled=True)
    normed = rms_scale(hidden_in, norm_gain).astype(jnp.bfloat16)
    scores = jnp.dot(normed, router_weight, preferred_element_type=jnp.float32)
    chosen = routes[:, :, None] == jnp.arange(expert_count, dtype=jnp.int32)[None, None, :]
    picked = jnp.sum(jnp.where(chosen, scores[:, None, :], 0.0), -1)
    gate_values = jax.nn.softmax(picked, axis=-1).astype(jnp.bfloat16)
    gate_table = jnp.sum(jnp.where(chosen, gate_values.astype(jnp.float32)[:, :, None], 0.0), 1)
    member = jnp.sum(chosen.astype(jnp.int32), 1)
    slot_rank = jnp.cumsum(member, 0) - member
    slot_base = lax.rem(lane_index, 2) * slot_count
    slot_hit = (member[:, :, None] == 1) & (
        slot_rank[:, :, None] == slot_base + jnp.arange(slot_count, dtype=jnp.int32)[None, None, :]
    )
    owner_expert = (
        jnp.arange(group_count, dtype=jnp.int32) * lane_count + lane_index
    ) // SPLITS
    pick_expert = (
        owner_expert[:, None] == jnp.arange(expert_count, dtype=jnp.int32)[None, :]
    ).astype(jnp.bfloat16)
    dispatch = jnp.einsum(
        "te,nec->tcn",
        pick_expert,
        slot_hit.astype(jnp.bfloat16),
        preferred_element_type=jnp.float32,
    ).astype(jnp.bfloat16)
    outgoing = jnp.einsum(
        "tcn,nd->tcd", dispatch, normed, preferred_element_type=jnp.float32
    ).astype(jnp.bfloat16)
    expert_gate = jnp.einsum(
        "te,ne->tn",
        pick_expert,
        gate_table.astype(jnp.bfloat16),
        preferred_element_type=jnp.float32,
    )
    combine = (dispatch.astype(jnp.float32) * expert_gate[:, None, :]).astype(jnp.bfloat16)
    own_up, own_down = w_gate_up[0], w_down[0]
    rows, pair_up, pair_down = dispatch_rows(outgoing, own_up, own_down, 1)
    rows = rows.reshape(group_count * slot_count, width)

    def block(up, down):
        lifted = jnp.dot(rows, up, preferred_element_type=jnp.float32)
        active = (
            jax.nn.silu(lifted[:, :unit_count]) * lifted[:, unit_count:]
        ).astype(jnp.bfloat16)
        return jnp.dot(active, down, preferred_element_type=jnp.float32)

    result = (block(own_up, own_down) + block(pair_up, pair_down)).astype(jnp.bfloat16)
    returned = exchange(result.reshape(group_count, slot_count, width), "gx", 2)
    partial_value = jnp.einsum(
        "tcn,tcd->nd", combine, returned, preferred_element_type=jnp.float32
    ).astype(jnp.bfloat16)
    pieces = exchange(partial_value.reshape(lane_count, share_rows, width), "gy", 3)
    summed = jnp.sum(pieces.astype(jnp.float32), 0)
    residual = lax.dynamic_slice_in_dim(hidden_in, lane_index * share_rows, share_rows, 0)
    layer_out = (residual.astype(jnp.float32) + summed).astype(jnp.bfloat16)
    final_states = rms_scale(layer_out, final_gain).astype(jnp.bfloat16)
    gathered = relay_gather(final_states, 4).reshape(group_count * share_rows, width)
    target_grid = targets.reshape(group_count, tok_rows)
    logits = jnp.dot(gathered, head_full, preferred_element_type=jnp.float32)
    offset = group_index * columns
    own_targets = lax.dynamic_slice_in_dim(
        target_grid, lane_index * share_rows, share_rows, 1
    ).reshape(group_count * share_rows)
    target_hits = (offset + jnp.arange(columns, dtype=jnp.int32))[None, :] == own_targets[:, None]
    local_peak = jnp.max(logits, -1)
    shifted = logits - local_peak[:, None]
    weights = jnp.exp(shifted)
    local = jnp.stack(
        [
            local_peak,
            jnp.sum(weights, -1),
            jnp.sum(weights * shifted, -1),
            jnp.sum(jnp.where(target_hits, logits, 0.0), -1),
        ]
    )
    stats = exchange(local, "gx", 5, same=True)
    peaks, masses, spreads = stats[:, 0], stats[:, 1], stats[:, 2]
    peak_value = jnp.max(peaks, 0)
    below = peaks - peak_value[None, :]
    scale = jnp.exp(below)
    total_mass = jnp.sum(masses * scale, 0)
    spread = jnp.sum(scale * (spreads + below * masses), 0)
    log_mass = jnp.log(total_mass)
    logprob = jnp.sum(stats[:, 3], 0) - peak_value - log_mass
    entropy = log_mass - spread / total_mass
    return (logprob.reshape(group_count, share_rows), entropy.reshape(group_count, share_rows))


def solution(mesh):
    return jax.shard_map(
        shards,
        mesh=mesh,
        in_specs=(
            P("gx", None),
            P(),
            P(),
            P("gx", None),
            P(("gx", "gy"), None, None),
            P(("gx", "gy"), None, None),
            P(),
            P("gy", "gx"),
            P(),
        ),
        out_specs=(P(None, "gy"), P(None, "gy")),
        check_vma=False,
    )
```

```python
import functools

import jax
import jax.numpy as jnp
from jax import lax
from jax.experimental import pallas as pl
from jax.experimental.pallas import tpu as pltpu
from jax.sharding import PartitionSpec as P

SPLITS = 8
X_CHIPS = 4

NORM_EPSILON = 1e-06

VMEM = pl.BlockSpec(memory_space=pltpu.VMEM)
ANY = pl.BlockSpec(memory_space=pl.ANY)


def rms_scale(values, gain_vector):
    widened = values.astype(jnp.float32)
    return (
        widened
        * lax.rsqrt(jnp.mean(widened * widened, -1, keepdims=True) + NORM_EPSILON)
        * gain_vector.astype(jnp.float32)
    )


def remote(src, dst, send_sem, recv_sem, device):
    return pltpu.make_async_remote_copy(
        src_ref=src,
        dst_ref=dst,
        send_sem=send_sem,
        recv_sem=recv_sem,
        device_id=device,
        device_id_type=pl.DeviceIdType.MESH,
    )


def greet(devices):
    barrier = pltpu.get_barrier_semaphore()
    for device in devices:
        pl.semaphore_signal(
            barrier, inc=1, device_id=device, device_id_type=pl.DeviceIdType.MESH
        )
    pl.semaphore_wait(barrier, len(devices))


def offsets(axis, count):
    if axis == "gy":
        steps = []
        for z in range(1, count // 2 + 1):
            steps += [z] if 2 * z == count else [z, -z]
        return steps
    y_chips = count // X_CHIPS
    steps = []
    for y in range(0, y_chips // 2 + 1):
        for x in range(X_CHIPS):
            for sign in (1, -1):
                if (y == 0 or 2 * y == y_chips) and sign == -1:
                    continue
                if y or x:
                    steps.append((sign * y, x))
    return steps


def partners(axis, count, me):
    if axis == "gy":
        return [lax.rem(me + step + count, count) for step in offsets(axis, count)]
    y_chips = count // X_CHIPS
    y, x = me // X_CHIPS, lax.rem(me, X_CHIPS)
    return [
        lax.rem(y + dy + y_chips, y_chips) * X_CHIPS + lax.rem(x + dx, X_CHIPS)
        for dy, dx in offsets(axis, count)
    ]


def exchange_kernel(axis, same, count, *refs):
    src, out, send_sem, recv_sem, own_sem = refs
    me = lax.axis_index(axis)
    core = 0
    if axis == "gy":
        me, core = me // 2, lax.rem(me, 2)

    def device(other):
        return {axis: 2 * other + core if axis == "gy" else other}

    others = partners(axis, count, me)
    greet([device(other) for other in others])
    copies = [
        remote(
            src if same else src.at[other],
            out.at[me],
            send_sem.at[other],
            recv_sem.at[me],
            device(other),
        )
        for other in others
    ]
    for copy in copies:
        copy.start()
    own = pltpu.make_async_copy(src if same else src.at[me], out.at[me], own_sem)
    own.start()
    own.wait()
    for other in others:
        remote(
            src if same else src.at[other],
            out.at[other],
            send_sem.at[other],
            recv_sem.at[other],
            device(other),
        ).wait_recv()
    for copy in copies:
        copy.wait_send()


def exchange(values, axis, collective_id, same=False):
    count = lax.axis_size(axis) // (2 if axis == "gy" else 1)
    shape = (count,) + values.shape if same else values.shape
    return pl.pallas_call(
        functools.partial(exchange_kernel, axis, same, count),
        out_shape=jax.ShapeDtypeStruct(shape, values.dtype),
        in_specs=[VMEM],
        out_specs=VMEM,
        scratch_shapes=[
            pltpu.SemaphoreType.DMA((count,)),
            pltpu.SemaphoreType.DMA((count,)),
            pltpu.SemaphoreType.DMA,
        ],
        compiler_params=pltpu.CompilerParams(collective_id=collective_id, has_side_effects=True),
        cost_estimate=pl.CostEstimate(
            flops=0, bytes_accessed=40_000_000, transcendentals=0
        ),
    )(values)


def relay_roles(count, me):
    y_chips = count // X_CHIPS
    y, x = me // X_CHIPS, lax.rem(me, X_CHIPS)

    def at(row, column):
        return lax.rem(row + y_chips, y_chips) * X_CHIPS + lax.rem(column + X_CHIPS, X_CHIPS)

    half = y_chips // 2
    sends = [(at(y + half, x + dx), at(y - 1, x + dx)) for dx in (1, 3)]
    serves = [(at(y + 1, x - dx), at(y + 1 + half, x)) for dx in (1, 3)]
    direct = [
        at(y + dy, x + dx)
        for dy, dx in offsets("gx", count)
        if not (dy == half and dx in (1, 3))
    ]
    everyone = partners("gx", count, me)
    return sends, serves, direct, everyone


def dispatch_kernel(count, *refs):
    (src, up, down, out, other_up, other_down) = refs[:6]
    (held, send_sem, recv_sem, own_sem, pair_sems, relay_sems) = refs[6:]
    me = lax.axis_index("gx")
    lane = lax.axis_index("gy")
    sends, serves, direct, everyone = relay_roles(count, me)
    pair = {"gy": lane + 1 - 2 * lax.rem(lane, 2)}
    greet([pair] + [{"gx": other} for other in everyone])
    sent = []

    def send(copy):
        copy.start()
        sent.append(copy)

    for k, (target, relay) in enumerate(sends):
        send(
            remote(
                src.at[target], held.at[k], send_sem.at[target], relay_sems.at[k], {"gx": relay}
            )
        )
    for other in direct:
        send(
            remote(
                src.at[other], out.at[me], send_sem.at[other], recv_sem.at[me], {"gx": other}
            )
        )
    swaps = [
        remote(up, other_up, pair_sems.at[0], pair_sems.at[1], pair),
        remote(down, other_down, pair_sems.at[2], pair_sems.at[3], pair),
    ]
    for copy in swaps:
        copy.start()
    own = pltpu.make_async_copy(src.at[me], out.at[me], own_sem)
    own.start()
    for k, (source, target) in enumerate(serves):
        remote(
            held.at[k], held.at[k], relay_sems.at[2 + k], relay_sems.at[k], {"gx": target}
        ).wait_recv()
        send(
            remote(
                held.at[k], out.at[source], relay_sems.at[2 + k], recv_sem.at[source], {"gx": target}
            )
        )
    own.wait()
    for other in everyone:
        remote(
            src.at[other], out.at[other], send_sem.at[other], recv_sem.at[other], {"gx": other}
        ).wait_recv()
    for copy in sent:
        copy.wait_send()
    for copy in swaps:
        copy.wait()


def dispatch_rows(values, up, down, collective_id):
    count = lax.axis_size("gx")
    return pl.pallas_call(
        functools.partial(dispatch_kernel, count),
        out_shape=(
            jax.ShapeDtypeStruct(values.shape, values.dtype),
            jax.ShapeDtypeStruct(up.shape, up.dtype),
            jax.ShapeDtypeStruct(down.shape, down.dtype),
        ),
        in_specs=[VMEM, ANY, ANY],
        out_specs=(VMEM, ANY, ANY),
        scratch_shapes=[
            pltpu.VMEM((2,) + values.shape[1:], values.dtype),
            pltpu.SemaphoreType.DMA((count,)),
            pltpu.SemaphoreType.DMA((count,)),
            pltpu.SemaphoreType.DMA,
            pltpu.SemaphoreType.DMA((4,)),
            pltpu.SemaphoreType.DMA((4,)),
        ],
        compiler_params=pltpu.CompilerParams(collective_id=collective_id, has_side_effects=True),
        cost_estimate=pl.CostEstimate(
            flops=0, bytes_accessed=100_000_000, transcendentals=0
        ),
    )(values, up, down)


def return_kernel(count, *refs):
    (src, out, held, send_sem, recv_sem, own_sem, relay_sems) = refs
    me = lax.axis_index("gx")
    lane = lax.axis_index("gy")
    core = lax.rem(lane, 2)
    first = lane - core
    wide = src.shape[2] // 2
    sends, serves, direct, everyone = relay_roles(count, me)
    pair = {"gy": first + 1 - core}
    greet([pair] + [{"gx": other, "gy": first + c} for other in everyone for c in range(2)])
    sent = []

    def send(copy):
        copy.start()
        sent.append(copy)

    def half(c):
        return pl.ds(pl.multiple_of(c * wide, 128), wide)

    for k, (target, relay) in enumerate(sends):
        send(
            remote(
                src.at[target],
                held.at[k],
                send_sem.at[target, 0],
                relay_sems.at[k],
                {"gx": relay},
            )
        )
    for other in direct:
        for c in range(2):
            send(
                remote(
                    src.at[other, :, half(c)],
                    out.at[me, core],
                    send_sem.at[other, c],
                    recv_sem.at[me, core],
                    {"gx": other, "gy": first + c},
                )
            )
    send(
        remote(
            src.at[me, :, half(1 - core)],
            out.at[me, core],
            send_sem.at[me, 0],
            recv_sem.at[me, core],
            pair,
        )
    )
    own = pltpu.make_async_copy(src.at[me, :, half(core)], out.at[me, core], own_sem)
    own.start()
    for k, (source, target) in enumerate(serves):
        remote(
            held.at[k], held.at[k], relay_sems.at[2 + k], relay_sems.at[k], {"gx": target}
        ).wait_recv()
        for c in range(2):
            send(
                remote(
                    held.at[k, :, half(c)],
                    out.at[source, core],
                    relay_sems.at[2 + 2 * k + c],
                    recv_sem.at[source, core],
                    {"gx": target, "gy": first + c},
                )
            )
    own.wait()
    for other in everyone:
        for c in range(2):
            remote(
                src.at[other, :, half(c)],
                out.at[other, c],
                send_sem.at[other, c],
                recv_sem.at[other, c],
                {"gx": other},
            ).wait_recv()
    remote(
        src.at[me, :, half(core)],
        out.at[me, 1 - core],
        send_sem.at[me, 0],
        recv_sem.at[me, 1 - core],
        pair,
    ).wait_recv()
    for copy in sent:
        copy.wait_send()


def return_rows(values, collective_id):
    count = lax.axis_size("gx")
    slots, width = values.shape[1:]
    return pl.pallas_call(
        functools.partial(return_kernel, count),
        out_shape=jax.ShapeDtypeStruct((count, 2, slots, width // 2), values.dtype),
        in_specs=[VMEM],
        out_specs=VMEM,
        scratch_shapes=[
            pltpu.VMEM((2, slots, width), values.dtype),
            pltpu.SemaphoreType.DMA((count, 2)),
            pltpu.SemaphoreType.DMA((count, 2)),
            pltpu.SemaphoreType.DMA,
            pltpu.SemaphoreType.DMA((6,)),
        ],
        compiler_params=pltpu.CompilerParams(collective_id=collective_id, has_side_effects=True),
        cost_estimate=pl.CostEstimate(
            flops=0, bytes_accessed=40_000_000, transcendentals=0
        ),
    )(values)


def pair_kernel(src, out, send_sem, recv_sem, own_sem):
    lane = lax.axis_index("gy")
    core = lax.rem(lane, 2)
    pair = {"gy": lane + 1 - 2 * core}
    greet([pair])
    copy = remote(src.at[1 - core], out.at[core], send_sem, recv_sem, pair)
    copy.start()
    own = pltpu.make_async_copy(src.at[core], out.at[core], own_sem)
    own.start()
    own.wait()
    copy.wait_send()
    remote(src.at[core], out.at[1 - core], send_sem, recv_sem, pair).wait_recv()


def pair_swap(values, collective_id):
    return pl.pallas_call(
        pair_kernel,
        out_shape=jax.ShapeDtypeStruct(values.shape, values.dtype),
        in_specs=[VMEM],
        out_specs=VMEM,
        scratch_shapes=[pltpu.SemaphoreType.DMA] * 3,
        compiler_params=pltpu.CompilerParams(collective_id=collective_id, has_side_effects=True),
    )(values)


def relay_kernel(count, *refs):
    src, out, send_sem, recv_sem, own_sem = refs
    me = lax.axis_index("gx")
    y_chips = count // X_CHIPS
    y, x = me // X_CHIPS, lax.rem(me, X_CHIPS)

    def at(row, column):
        return lax.rem(row + y_chips, y_chips) * X_CHIPS + lax.rem(column, X_CHIPS)

    above, below = at(y + 1, x), at(y - 1, x)
    right, left = at(y, x + 1), at(y, x + 3)
    greet([{"gx": other} for other in (above, below, right, left)])
    sent = []

    def send(block, source, target):
        copy = remote(
            source, out.at[block], send_sem.at[len(sent)], recv_sem.at[block], {"gx": target}
        )
        copy.start()
        sent.append(copy)

    def arrived(block):
        remote(
            src, out.at[block], send_sem.at[0], recv_sem.at[block], {"gx": above}
        ).wait_recv()

    def across(k):
        near, far = (x + 3, right) if k % 2 == 0 else (x + 1, left)
        block = at(y + k, near)
        arrived(block)
        send(block, out.at[block], far)

    send(me, src, above)
    send(me, src, below)
    send(me, src, right)
    send(me, src, left)
    own = pltpu.make_async_copy(src, out.at[me], own_sem)
    own.start()
    half = y_chips // 2
    order = [0]
    for step in range(1, half + 1):
        order.append(y_chips - step)
        if step < half:
            order.append(step)
    for i, k in enumerate(order):
        if k:
            block = at(y + k, x)
            arrived(block)
            if half < k:
                send(block, out.at[block], above)
            elif k < half - 1:
                send(block, out.at[block], below)
            send(block, out.at[block], right)
            send(block, out.at[block], left)
        if i >= 1:
            across(order[i - 1])
    across(order[-1])
    for k in order:
        arrived(at(y + k, x + (1 if k % 2 == 0 else 3)))
        arrived(at(y + k, x + 2))
    own.wait()
    for copy in sent:
        copy.wait_send()


def relay_gather(values, collective_id):
    count = lax.axis_size("gx")
    return pl.pallas_call(
        functools.partial(relay_kernel, count),
        out_shape=jax.ShapeDtypeStruct((count,) + values.shape, values.dtype),
        in_specs=[VMEM],
        out_specs=VMEM,
        scratch_shapes=[
            pltpu.SemaphoreType.DMA((count,)),
            pltpu.SemaphoreType.DMA((count,)),
            pltpu.SemaphoreType.DMA,
        ],
        compiler_params=pltpu.CompilerParams(collective_id=collective_id, has_side_effects=True),
        cost_estimate=pl.CostEstimate(
            flops=0, bytes_accessed=40_000_000, transcendentals=0
        ),
    )(values)


def shards(
    hidden_in, norm_gain, router_weight, routes, w_gate_up, w_down, final_gain, head_weight, targets
):
    tok_rows = hidden_in.shape[0]
    width = hidden_in.shape[1]
    group_count = lax.axis_size("gx")
    lane_count = lax.axis_size("gy")
    group_index = lax.axis_index("gx")
    lane_index = lax.axis_index("gy")
    expert_count = router_weight.shape[1]
    unit_count = w_down.shape[1]
    slot_count = tok_rows // 8
    half_slots = slot_count // 2
    share_rows = tok_rows // lane_count
    columns = head_weight.shape[1]
    head_full = lax.all_gather(head_weight, "gy", axis=0, tiled=True)
    normed = rms_scale(hidden_in, norm_gain).astype(jnp.bfloat16)
    scores = jnp.dot(normed, router_weight, preferred_element_type=jnp.float32)
    chosen = routes[:, :, None] == jnp.arange(expert_count, dtype=jnp.int32)[None, None, :]
    picked = jnp.sum(jnp.where(chosen, scores[:, None, :], 0.0), -1)
    gate_values = jax.nn.softmax(picked, axis=-1).astype(jnp.bfloat16)
    gate_table = jnp.sum(jnp.where(chosen, gate_values.astype(jnp.float32)[:, :, None], 0.0), 1)
    member = jnp.sum(chosen.astype(jnp.int32), 1)
    slot_rank = jnp.cumsum(member, 0) - member
    slot_hit = (member[:, :, None] == 1) & (
        slot_rank[:, :, None] == jnp.arange(slot_count, dtype=jnp.int32)[None, None, :]
    )
    owner_expert = (
        jnp.arange(group_count, dtype=jnp.int32) * lane_count + lane_index
    ) // SPLITS
    pick_expert = (
        owner_expert[:, None] == jnp.arange(expert_count, dtype=jnp.int32)[None, :]
    ).astype(jnp.bfloat16)
    dispatch = jnp.einsum(
        "te,nec->tcn",
        pick_expert,
        slot_hit.astype(jnp.bfloat16),
        preferred_element_type=jnp.float32,
    ).astype(jnp.bfloat16)
    core = lax.rem(lane_index, 2)
    own_slots = lax.dynamic_slice_in_dim(dispatch, core * half_slots, half_slots, 1)
    outgoing = jnp.einsum(
        "tcn,nd->tcd", own_slots, normed, preferred_element_type=jnp.float32
    ).astype(jnp.bfloat16)
    expert_gate = jnp.einsum(
        "te,ne->tn",
        pick_expert,
        gate_table.astype(jnp.bfloat16),
        preferred_element_type=jnp.float32,
    )
    combine = (dispatch.astype(jnp.float32) * expert_gate[:, None, :]).astype(jnp.bfloat16)
    own_up, own_down = w_gate_up[0], w_down[0]
    rows, pair_up, pair_down = dispatch_rows(outgoing, own_up, own_down, 1)
    rows = rows.reshape(group_count * half_slots, width)

    def block(up, down):
        lifted = jnp.dot(rows, up, preferred_element_type=jnp.float32)
        active = (
            jax.nn.silu(lifted[:, :unit_count]) * lifted[:, unit_count:]
        ).astype(jnp.bfloat16)
        return jnp.dot(active, down, preferred_element_type=jnp.float32)

    result = (block(own_up, own_down) + block(pair_up, pair_down)).astype(jnp.bfloat16)
    returned = return_rows(result.reshape(group_count, half_slots, width), 2)
    partial_value = jnp.einsum(
        "tcn,tcd->nd",
        combine,
        returned.reshape(group_count, slot_count, width // 2),
        preferred_element_type=jnp.float32,
    ).astype(jnp.bfloat16)
    chips = lane_count // 2
    pieces = exchange(partial_value.reshape(chips, 2 * share_rows, width // 2), "gy", 3)
    halves = pair_swap(
        jnp.sum(pieces.astype(jnp.float32), 0).reshape(2, share_rows, width // 2), 6
    )
    summed = jnp.concatenate([halves[0], halves[1]], axis=-1)
    residual = lax.dynamic_slice_in_dim(hidden_in, lane_index * share_rows, share_rows, 0)
    layer_out = (residual.astype(jnp.float32) + summed).astype(jnp.bfloat16)
    final_states = rms_scale(layer_out, final_gain).astype(jnp.bfloat16)
    gathered = relay_gather(final_states, 4).reshape(group_count * share_rows, width)
    target_grid = targets.reshape(group_count, tok_rows)
    logits = jnp.dot(gathered, head_full, preferred_element_type=jnp.float32)
    offset = group_index * columns
    own_targets = lax.dynamic_slice_in_dim(
        target_grid, lane_index * share_rows, share_rows, 1
    ).reshape(group_count * share_rows)
    target_hits = (offset + jnp.arange(columns, dtype=jnp.int32))[None, :] == own_targets[:, None]
    local_peak = jnp.max(logits, -1)
    shifted = logits - local_peak[:, None]
    weights = jnp.exp(shifted)
    local = jnp.stack(
        [
            local_peak,
            jnp.sum(weights, -1),
            jnp.sum(weights * shifted, -1),
            jnp.sum(jnp.where(target_hits, logits, 0.0), -1),
        ]
    )
    stats = exchange(local, "gx", 5, same=True)
    peaks, masses, spreads = stats[:, 0], stats[:, 1], stats[:, 2]
    peak_value = jnp.max(peaks, 0)
    below = peaks - peak_value[None, :]
    scale = jnp.exp(below)
    total_mass = jnp.sum(masses * scale, 0)
    spread = jnp.sum(scale * (spreads + below * masses), 0)
    log_mass = jnp.log(total_mass)
    logprob = jnp.sum(stats[:, 3], 0) - peak_value - log_mass
    entropy = log_mass - spread / total_mass
    return (logprob.reshape(group_count, share_rows), entropy.reshape(group_count, share_rows))


def solution(mesh):
    return jax.shard_map(
        shards,
        mesh=mesh,
        in_specs=(
            P("gx", None),
            P(),
            P(),
            P("gx", None),
            P(("gx", "gy"), None, None),
            P(("gx", "gy"), None, None),
            P(),
            P("gy", "gx"),
            P(),
        ),
        out_specs=(P(None, "gy"), P(None, "gy")),
        check_vma=False,
    )
```

```python
import functools

import jax
import jax.numpy as jnp
from jax import lax
from jax.experimental import pallas as pl
from jax.experimental.pallas import tpu as pltpu
from jax.sharding import PartitionSpec as P

SPLITS = 8
X_CHIPS = 4

NORM_EPSILON = 1e-06

VMEM = pl.BlockSpec(memory_space=pltpu.VMEM)


def rms_scale(values, gain_vector):
    widened = values.astype(jnp.float32)
    return (
        widened
        * lax.rsqrt(jnp.mean(widened * widened, -1, keepdims=True) + NORM_EPSILON)
        * gain_vector.astype(jnp.float32)
    )


def remote(src, dst, send_sem, recv_sem, device):
    return pltpu.make_async_remote_copy(
        src_ref=src,
        dst_ref=dst,
        send_sem=send_sem,
        recv_sem=recv_sem,
        device_id=device,
        device_id_type=pl.DeviceIdType.MESH,
    )


def greet(devices):
    barrier = pltpu.get_barrier_semaphore()
    for device in devices:
        pl.semaphore_signal(
            barrier, inc=1, device_id=device, device_id_type=pl.DeviceIdType.MESH
        )
    pl.semaphore_wait(barrier, len(devices))


def offsets(axis, count):
    if axis == "gy":
        steps = []
        for z in range(1, count // 2 + 1):
            steps += [z] if 2 * z == count else [z, -z]
        return steps
    y_chips = count // X_CHIPS
    steps = []
    for y in range(0, y_chips // 2 + 1):
        for x in range(X_CHIPS):
            for sign in (1, -1):
                if (y == 0 or 2 * y == y_chips) and sign == -1:
                    continue
                if y or x:
                    steps.append((sign * y, x))
    return steps


def partners(axis, count, me):
    if axis == "gy":
        return [lax.rem(me + step + count, count) for step in offsets(axis, count)]
    y_chips = count // X_CHIPS
    y, x = me // X_CHIPS, lax.rem(me, X_CHIPS)
    return [
        lax.rem(y + dy + y_chips, y_chips) * X_CHIPS + lax.rem(x + dx, X_CHIPS)
        for dy, dx in offsets(axis, count)
    ]


def exchange_kernel(axis, same, count, *refs):
    src, out, send_sem, recv_sem, own_sem = refs
    me = lax.axis_index(axis)
    core = 0
    if axis == "gy":
        me, core = me // 2, lax.rem(me, 2)

    def device(other):
        return {axis: 2 * other + core if axis == "gy" else other}

    others = partners(axis, count, me)
    greet([device(other) for other in others])
    copies = [
        remote(
            src if same else src.at[other],
            out.at[me],
            send_sem.at[other],
            recv_sem.at[me],
            device(other),
        )
        for other in others
    ]
    for copy in copies:
        copy.start()
    own = pltpu.make_async_copy(src if same else src.at[me], out.at[me], own_sem)
    own.start()
    own.wait()
    for other in others:
        remote(
            src if same else src.at[other],
            out.at[other],
            send_sem.at[other],
            recv_sem.at[other],
            device(other),
        ).wait_recv()
    for copy in copies:
        copy.wait_send()


def exchange(values, axis, collective_id, same=False):
    count = lax.axis_size(axis) // (2 if axis == "gy" else 1)
    shape = (count,) + values.shape if same else values.shape
    return pl.pallas_call(
        functools.partial(exchange_kernel, axis, same, count),
        out_shape=jax.ShapeDtypeStruct(shape, values.dtype),
        in_specs=[VMEM],
        out_specs=VMEM,
        scratch_shapes=[
            pltpu.SemaphoreType.DMA((count,)),
            pltpu.SemaphoreType.DMA((count,)),
            pltpu.SemaphoreType.DMA,
        ],
        compiler_params=pltpu.CompilerParams(collective_id=collective_id, has_side_effects=True),
        cost_estimate=pl.CostEstimate(
            flops=0, bytes_accessed=40_000_000, transcendentals=0
        ),
    )(values)


def expert_kernel(count, *refs):
    (src, up, down, out, rows, result, other_up, other_down) = refs[:8]
    (send_sem, recv_sem, back_send, back_recv, own_sems, pair_sems) = refs[8:]
    me = lax.axis_index("gx")
    lane = lax.axis_index("gy")
    core = lax.rem(lane, 2)
    first = lane - core
    pair = {"gy": first + 1 - core}
    slots, width = src.shape[1:]
    wide = width // 2
    units = down.shape[0]
    y_chips = count // X_CHIPS
    steps = [(0, 0)] + [(dy % y_chips, dx) for dy, dx in offsets("gx", count)]
    y, x = me // X_CHIPS, lax.rem(me, X_CHIPS)
    peers = [
        lax.rem(y + dy, y_chips) * X_CHIPS + lax.rem(x + dx, X_CHIPS) for dy, dx in steps
    ]
    mirror = [
        steps.index(((y_chips - dy) % y_chips, (X_CHIPS - dx) % X_CHIPS)) for dy, dx in steps
    ]
    greet([pair] + [{"gx": other, "gy": first + c} for other in peers[1:] for c in range(2)])

    def half(c):
        return pl.ds(pl.multiple_of(c * wide, 128), wide)

    swaps = [
        remote(up, other_up, pair_sems.at[0], pair_sems.at[1], pair),
        remote(down, other_down, pair_sems.at[2], pair_sems.at[3], pair),
    ]
    for copy in swaps:
        copy.start()
    sent = [
        remote(
            src.at[peers[r]],
            rows.at[mirror[r]],
            send_sem.at[r],
            recv_sem.at[mirror[r]],
            {"gx": peers[r]},
        )
        for r in range(1, count)
    ]
    for copy in sent:
        copy.start()
    own = pltpu.make_async_copy(src.at[me], rows.at[0], own_sems.at[0])
    own.start()
    own.wait()
    backs = []

    def give_back(r):
        for c in range(2):
            if r:
                copy = remote(
                    result.at[r, :, half(c)],
                    out.at[me, core],
                    back_send.at[r, c],
                    back_recv.at[mirror[r], core],
                    {"gx": peers[r], "gy": first + c},
                )
                copy.start()
                backs.append(copy)
        if not r:
            copy = remote(
                result.at[0, :, half(1 - core)],
                out.at[me, core],
                back_send.at[0, 0],
                back_recv.at[0, core],
                pair,
            )
            copy.start()
            backs.append(copy)
            pltpu.make_async_copy(
                result.at[0, :, half(core)], out.at[me, core], own_sems.at[1]
            ).start()

    def block(chunk, up_ref, down_ref):
        lifted = jnp.dot(chunk, up_ref[...], preferred_element_type=jnp.float32)
        gate = lifted[:, :units]
        active = gate / (1.0 + jnp.exp(-gate)) * lifted[:, units:]
        return jnp.dot(
            active.astype(jnp.bfloat16), down_ref[...], preferred_element_type=jnp.float32
        )

    size = 8
    for base in range(0, count, size):
        for r in range(max(base, 1), base + size):
            remote(
                src.at[peers[r]], rows.at[r], send_sem.at[r], recv_sem.at[r], {"gx": peers[r]}
            ).wait_recv()
        if base:
            for r in range(base - size, base):
                give_back(r)
        else:
            for copy in swaps:
                copy.wait_recv()
        chunk = rows[pl.ds(base, size)].reshape(size * slots, width)
        total = block(chunk, up, down) + block(chunk, other_up, other_down)
        result[pl.ds(base, size)] = total.astype(jnp.bfloat16).reshape(size, slots, width)
    for copy in sent + swaps:
        copy.wait_send()
    for r in range(count - size, count):
        give_back(r)
    pltpu.make_async_copy(
        result.at[0, :, half(core)], out.at[me, core], own_sems.at[1]
    ).wait()
    for r in range(1, count):
        for c in range(2):
            remote(
                result.at[r, :, half(c)],
                out.at[peers[r], c],
                back_send.at[r, c],
                back_recv.at[r, c],
                {"gx": peers[r]},
            ).wait_recv()
    remote(
        result.at[0, :, half(core)],
        out.at[me, 1 - core],
        back_send.at[0, 0],
        back_recv.at[0, 1 - core],
        pair,
    ).wait_recv()
    for copy in backs:
        copy.wait_send()


def through_experts(values, up, down, collective_id):
    count = lax.axis_size("gx")
    slots, width = values.shape[1:]
    return pl.pallas_call(
        functools.partial(expert_kernel, count),
        out_shape=jax.ShapeDtypeStruct((count, 2, slots, width // 2), values.dtype),
        in_specs=[VMEM, VMEM, VMEM],
        out_specs=VMEM,
        scratch_shapes=[
            pltpu.VMEM(values.shape, values.dtype),
            pltpu.VMEM(values.shape, values.dtype),
            pltpu.VMEM(up.shape, up.dtype),
            pltpu.VMEM(down.shape, down.dtype),
            pltpu.SemaphoreType.DMA((count,)),
            pltpu.SemaphoreType.DMA((count,)),
            pltpu.SemaphoreType.DMA((count, 2)),
            pltpu.SemaphoreType.DMA((count, 2)),
            pltpu.SemaphoreType.DMA((2,)),
            pltpu.SemaphoreType.DMA((4,)),
        ],
        compiler_params=pltpu.CompilerParams(
            collective_id=collective_id, has_side_effects=True, vmem_limit_bytes=40 * 2**20
        ),
        cost_estimate=pl.CostEstimate(
            flops=0, bytes_accessed=200_000_000, transcendentals=0
        ),
    )(values, up, down)


def pair_kernel(src, out, send_sem, recv_sem, own_sem):
    lane = lax.axis_index("gy")
    core = lax.rem(lane, 2)
    pair = {"gy": lane + 1 - 2 * core}
    greet([pair])
    copy = remote(src.at[1 - core], out.at[core], send_sem, recv_sem, pair)
    copy.start()
    own = pltpu.make_async_copy(src.at[core], out.at[core], own_sem)
    own.start()
    own.wait()
    copy.wait_send()
    remote(src.at[core], out.at[1 - core], send_sem, recv_sem, pair).wait_recv()


def pair_swap(values, collective_id):
    return pl.pallas_call(
        pair_kernel,
        out_shape=jax.ShapeDtypeStruct(values.shape, values.dtype),
        in_specs=[VMEM],
        out_specs=VMEM,
        scratch_shapes=[pltpu.SemaphoreType.DMA] * 3,
        compiler_params=pltpu.CompilerParams(collective_id=collective_id, has_side_effects=True),
    )(values)


def relay_kernel(count, *refs):
    src, out, send_sem, recv_sem, own_sem = refs
    me = lax.axis_index("gx")
    y_chips = count // X_CHIPS
    y, x = me // X_CHIPS, lax.rem(me, X_CHIPS)

    def at(row, column):
        return lax.rem(row + y_chips, y_chips) * X_CHIPS + lax.rem(column, X_CHIPS)

    above, below = at(y + 1, x), at(y - 1, x)
    right, left = at(y, x + 1), at(y, x + 3)
    greet([{"gx": other} for other in (above, below, right, left)])
    sent = []

    def send(block, source, target):
        copy = remote(
            source, out.at[block], send_sem.at[len(sent)], recv_sem.at[block], {"gx": target}
        )
        copy.start()
        sent.append(copy)

    def arrived(block):
        remote(
            src, out.at[block], send_sem.at[0], recv_sem.at[block], {"gx": above}
        ).wait_recv()

    def across(k):
        near, far = (x + 3, right) if k % 2 == 0 else (x + 1, left)
        block = at(y + k, near)
        arrived(block)
        send(block, out.at[block], far)

    send(me, src, above)
    send(me, src, below)
    send(me, src, right)
    send(me, src, left)
    own = pltpu.make_async_copy(src, out.at[me], own_sem)
    own.start()
    half = y_chips // 2
    order = [0]
    for step in range(1, half + 1):
        order.append(y_chips - step)
        if step < half:
            order.append(step)
    for i, k in enumerate(order):
        if k:
            block = at(y + k, x)
            arrived(block)
            if half < k:
                send(block, out.at[block], above)
            elif k < half - 1:
                send(block, out.at[block], below)
            send(block, out.at[block], right)
            send(block, out.at[block], left)
        if i >= 1:
            across(order[i - 1])
    across(order[-1])
    for k in order:
        arrived(at(y + k, x + (1 if k % 2 == 0 else 3)))
        arrived(at(y + k, x + 2))
    own.wait()
    for copy in sent:
        copy.wait_send()


def relay_gather(values, collective_id):
    count = lax.axis_size("gx")
    return pl.pallas_call(
        functools.partial(relay_kernel, count),
        out_shape=jax.ShapeDtypeStruct((count,) + values.shape, values.dtype),
        in_specs=[VMEM],
        out_specs=VMEM,
        scratch_shapes=[
            pltpu.SemaphoreType.DMA((count,)),
            pltpu.SemaphoreType.DMA((count,)),
            pltpu.SemaphoreType.DMA,
        ],
        compiler_params=pltpu.CompilerParams(collective_id=collective_id, has_side_effects=True),
        cost_estimate=pl.CostEstimate(
            flops=0, bytes_accessed=40_000_000, transcendentals=0
        ),
    )(values)


def shards(
    hidden_in, norm_gain, router_weight, routes, w_gate_up, w_down, final_gain, head_weight, targets
):
    tok_rows = hidden_in.shape[0]
    width = hidden_in.shape[1]
    group_count = lax.axis_size("gx")
    lane_count = lax.axis_size("gy")
    group_index = lax.axis_index("gx")
    lane_index = lax.axis_index("gy")
    expert_count = router_weight.shape[1]
    slot_count = tok_rows // 8
    half_slots = slot_count // 2
    share_rows = tok_rows // lane_count
    columns = head_weight.shape[1]
    head_full = lax.all_gather(head_weight, "gy", axis=0, tiled=True)
    normed = rms_scale(hidden_in, norm_gain).astype(jnp.bfloat16)
    scores = jnp.dot(normed, router_weight, preferred_element_type=jnp.float32)
    chosen = routes[:, :, None] == jnp.arange(expert_count, dtype=jnp.int32)[None, None, :]
    picked = jnp.sum(jnp.where(chosen, scores[:, None, :], 0.0), -1)
    gate_values = jax.nn.softmax(picked, axis=-1).astype(jnp.bfloat16)
    gate_table = jnp.sum(jnp.where(chosen, gate_values.astype(jnp.float32)[:, :, None], 0.0), 1)
    member = jnp.sum(chosen.astype(jnp.int32), 1)
    slot_rank = jnp.cumsum(member, 0) - member
    slot_hit = (member[:, :, None] == 1) & (
        slot_rank[:, :, None] == jnp.arange(slot_count, dtype=jnp.int32)[None, None, :]
    )
    owner_expert = (
        jnp.arange(group_count, dtype=jnp.int32) * lane_count + lane_index
    ) // SPLITS
    pick_expert = (
        owner_expert[:, None] == jnp.arange(expert_count, dtype=jnp.int32)[None, :]
    ).astype(jnp.bfloat16)
    dispatch = jnp.einsum(
        "te,nec->tcn",
        pick_expert,
        slot_hit.astype(jnp.bfloat16),
        preferred_element_type=jnp.float32,
    ).astype(jnp.bfloat16)
    core = lax.rem(lane_index, 2)
    own_slots = lax.dynamic_slice_in_dim(dispatch, core * half_slots, half_slots, 1)
    outgoing = jnp.einsum(
        "tcn,nd->tcd", own_slots, normed, preferred_element_type=jnp.float32
    ).astype(jnp.bfloat16)
    expert_gate = jnp.einsum(
        "te,ne->tn",
        pick_expert,
        gate_table.astype(jnp.bfloat16),
        preferred_element_type=jnp.float32,
    )
    combine = (dispatch.astype(jnp.float32) * expert_gate[:, None, :]).astype(jnp.bfloat16)
    returned = through_experts(outgoing, w_gate_up[0], w_down[0], 1)
    partial_value = jnp.einsum(
        "tcn,tcd->nd",
        combine,
        returned.reshape(group_count, slot_count, width // 2),
        preferred_element_type=jnp.float32,
    ).astype(jnp.bfloat16)
    chips = lane_count // 2
    pieces = exchange(partial_value.reshape(chips, 2 * share_rows, width // 2), "gy", 3)
    halves = pair_swap(
        jnp.sum(pieces.astype(jnp.float32), 0).reshape(2, share_rows, width // 2), 6
    )
    summed = jnp.concatenate([halves[0], halves[1]], axis=-1)
    residual = lax.dynamic_slice_in_dim(hidden_in, lane_index * share_rows, share_rows, 0)
    layer_out = (residual.astype(jnp.float32) + summed).astype(jnp.bfloat16)
    final_states = rms_scale(layer_out, final_gain).astype(jnp.bfloat16)
    gathered = relay_gather(final_states, 4).reshape(group_count * share_rows, width)
    target_grid = targets.reshape(group_count, tok_rows)
    logits = jnp.dot(gathered, head_full, preferred_element_type=jnp.float32)
    offset = group_index * columns
    own_targets = lax.dynamic_slice_in_dim(
        target_grid, lane_index * share_rows, share_rows, 1
    ).reshape(group_count * share_rows)
    target_hits = (offset + jnp.arange(columns, dtype=jnp.int32))[None, :] == own_targets[:, None]
    local_peak = jnp.max(logits, -1)
    shifted = logits - local_peak[:, None]
    weights = jnp.exp(shifted)
    local = jnp.stack(
        [
            local_peak,
            jnp.sum(weights, -1),
            jnp.sum(weights * shifted, -1),
            jnp.sum(jnp.where(target_hits, logits, 0.0), -1),
        ]
    )
    stats = exchange(local, "gx", 5, same=True)
    peaks, masses, spreads = stats[:, 0], stats[:, 1], stats[:, 2]
    peak_value = jnp.max(peaks, 0)
    below = peaks - peak_value[None, :]
    scale = jnp.exp(below)
    total_mass = jnp.sum(masses * scale, 0)
    spread = jnp.sum(scale * (spreads + below * masses), 0)
    log_mass = jnp.log(total_mass)
    logprob = jnp.sum(stats[:, 3], 0) - peak_value - log_mass
    entropy = log_mass - spread / total_mass
    return (logprob.reshape(group_count, share_rows), entropy.reshape(group_count, share_rows))


def solution(mesh):
    return jax.shard_map(
        shards,
        mesh=mesh,
        in_specs=(
            P("gx", None),
            P(),
            P(),
            P("gx", None),
            P(("gx", "gy"), None, None),
            P(("gx", "gy"), None, None),
            P(),
            P("gy", "gx"),
            P(),
        ),
        out_specs=(P(None, "gy"), P(None, "gy")),
        check_vma=False,
    )
```

```python
import functools

import jax
import jax.numpy as jnp
from jax import lax
from jax.experimental import pallas as pl
from jax.experimental.pallas import tpu as pltpu
from jax.sharding import PartitionSpec as P

SPLITS = 8
X_CHIPS = 4

NORM_EPSILON = 1e-06

VMEM = pl.BlockSpec(memory_space=pltpu.VMEM)


def rms_scale(values, gain_vector):
    widened = values.astype(jnp.float32)
    return (
        widened
        * lax.rsqrt(jnp.mean(widened * widened, -1, keepdims=True) + NORM_EPSILON)
        * gain_vector.astype(jnp.float32)
    )


def remote(src, dst, send_sem, recv_sem, device):
    return pltpu.make_async_remote_copy(
        src_ref=src,
        dst_ref=dst,
        send_sem=send_sem,
        recv_sem=recv_sem,
        device_id=device,
        device_id_type=pl.DeviceIdType.MESH,
    )


def greet(devices):
    barrier = pltpu.get_barrier_semaphore()
    for device in devices:
        pl.semaphore_signal(
            barrier, inc=1, device_id=device, device_id_type=pl.DeviceIdType.MESH
        )
    pl.semaphore_wait(barrier, len(devices))


def offsets(axis, count):
    if axis == "gy":
        steps = []
        for z in range(1, count // 2 + 1):
            steps += [z] if 2 * z == count else [z, -z]
        return steps
    y_chips = count // X_CHIPS
    steps = []
    for y in range(0, y_chips // 2 + 1):
        for x in range(X_CHIPS):
            for sign in (1, -1):
                if (y == 0 or 2 * y == y_chips) and sign == -1:
                    continue
                if y or x:
                    steps.append((sign * y, x))
    return steps


def partners(axis, count, me):
    if axis == "gy":
        return [lax.rem(me + step + count, count) for step in offsets(axis, count)]
    y_chips = count // X_CHIPS
    y, x = me // X_CHIPS, lax.rem(me, X_CHIPS)
    return [
        lax.rem(y + dy + y_chips, y_chips) * X_CHIPS + lax.rem(x + dx, X_CHIPS)
        for dy, dx in offsets(axis, count)
    ]


def exchange_kernel(axis, same, count, *refs):
    src, out, send_sem, recv_sem, own_sem = refs
    me = lax.axis_index(axis)
    core = 0
    if axis == "gy":
        me, core = me // 2, lax.rem(me, 2)

    def device(other):
        return {axis: 2 * other + core if axis == "gy" else other}

    others = partners(axis, count, me)
    greet([device(other) for other in others])
    copies = [
        remote(
            src if same else src.at[other],
            out.at[me],
            send_sem.at[other],
            recv_sem.at[me],
            device(other),
        )
        for other in others
    ]
    for copy in copies:
        copy.start()
    own = pltpu.make_async_copy(src if same else src.at[me], out.at[me], own_sem)
    own.start()
    own.wait()
    for other in others:
        remote(
            src if same else src.at[other],
            out.at[other],
            send_sem.at[other],
            recv_sem.at[other],
            device(other),
        ).wait_recv()
    for copy in copies:
        copy.wait_send()


def exchange(values, axis, collective_id, same=False):
    count = lax.axis_size(axis) // (2 if axis == "gy" else 1)
    shape = (count,) + values.shape if same else values.shape
    return pl.pallas_call(
        functools.partial(exchange_kernel, axis, same, count),
        out_shape=jax.ShapeDtypeStruct(shape, values.dtype),
        in_specs=[VMEM],
        out_specs=VMEM,
        scratch_shapes=[
            pltpu.SemaphoreType.DMA((count,)),
            pltpu.SemaphoreType.DMA((count,)),
            pltpu.SemaphoreType.DMA,
        ],
        compiler_params=pltpu.CompilerParams(collective_id=collective_id, has_side_effects=True),
        cost_estimate=pl.CostEstimate(
            flops=0, bytes_accessed=40_000_000, transcendentals=0
        ),
    )(values)


def expert_kernel(count, *refs):
    (src, up, down, out, rows, result, other_up, other_down) = refs[:8]
    (send_sem, recv_sem, back_send, back_recv, own_sems, pair_sems) = refs[8:14]
    (hand_send, hand_recv) = refs[14:]
    me = lax.axis_index("gx")
    lane = lax.axis_index("gy")
    core = lax.rem(lane, 2)
    first = lane - core
    pair = {"gy": first + 1 - core}
    side = lax.rem(lane // 2, 2)
    next_chip = {"gy": lane + 2 - 4 * side}
    slots, width = src.shape[1:]
    wide = width // 2
    units = down.shape[0]
    y_chips = count // X_CHIPS
    steps = [(0, 0)] + [(dy % y_chips, dx) for dy, dx in offsets("gx", count)]
    y, x = me // X_CHIPS, lax.rem(me, X_CHIPS)
    peers = [
        lax.rem(y + dy, y_chips) * X_CHIPS + lax.rem(x + dx, X_CHIPS) for dy, dx in steps
    ]
    mirror = [
        steps.index(((y_chips - dy) % y_chips, (X_CHIPS - dx) % X_CHIPS)) for dy, dx in steps
    ]
    greet(
        [pair, next_chip]
        + [{"gx": other, "gy": first + c} for other in peers[1:] for c in range(2)]
    )

    def half(c):
        return pl.ds(pl.multiple_of(c * wide, 128), wide)

    swaps = [
        remote(up, other_up, pair_sems.at[0], pair_sems.at[1], pair),
        remote(down, other_down, pair_sems.at[2], pair_sems.at[3], pair),
    ]
    for copy in swaps:
        copy.start()
    sent = [
        remote(
            src.at[peers[r], :, half(side)],
            rows.at[mirror[r], :, half(side)],
            send_sem.at[r],
            recv_sem.at[mirror[r]],
            {"gx": peers[r]},
        )
        for r in range(1, count)
    ]
    for copy in sent:
        copy.start()
    own = pltpu.make_async_copy(src.at[me], rows.at[0], own_sems.at[0])
    own.start()
    own.wait()
    backs = []

    def give_back(r):
        for c in range(2):
            if r:
                copy = remote(
                    result.at[r, :, half(c)],
                    out.at[me, core],
                    back_send.at[r, c],
                    back_recv.at[mirror[r], core],
                    {"gx": peers[r], "gy": first + c},
                )
                copy.start()
                backs.append(copy)
        if not r:
            copy = remote(
                result.at[0, :, half(1 - core)],
                out.at[me, core],
                back_send.at[0, 0],
                back_recv.at[0, core],
                pair,
            )
            copy.start()
            backs.append(copy)
            pltpu.make_async_copy(
                result.at[0, :, half(core)], out.at[me, core], own_sems.at[1]
            ).start()

    def block(chunk, up_ref, down_ref):
        lifted = jnp.dot(chunk, up_ref[...], preferred_element_type=jnp.float32)
        gate = lifted[:, :units]
        active = gate / (1.0 + jnp.exp(-gate)) * lifted[:, units:]
        return jnp.dot(
            active.astype(jnp.bfloat16), down_ref[...], preferred_element_type=jnp.float32
        )

    size = 8
    hands = []
    for base in range(0, count, size):
        for r in range(max(base, 1), base + size):
            remote(
                src.at[peers[r], :, half(side)],
                rows.at[r, :, half(side)],
                send_sem.at[r],
                recv_sem.at[r],
                {"gx": peers[r]},
            ).wait_recv()
            hand = remote(
                rows.at[r, :, half(side)],
                rows.at[r, :, half(side)],
                hand_send.at[r],
                hand_recv.at[r],
                next_chip,
            )
            hand.start()
            hands.append(hand)
        if base:
            for r in range(base - size, base):
                give_back(r)
        else:
            for copy in swaps:
                copy.wait_recv()
        for r in range(max(base, 1), base + size):
            remote(
                rows.at[r, :, half(side)],
                rows.at[r, :, half(1 - side)],
                hand_send.at[r],
                hand_recv.at[r],
                next_chip,
            ).wait_recv()
        chunk = rows[pl.ds(base, size)].reshape(size * slots, width)
        total = block(chunk, up, down) + block(chunk, other_up, other_down)
        result[pl.ds(base, size)] = total.astype(jnp.bfloat16).reshape(size, slots, width)
    for copy in sent + swaps + hands:
        copy.wait_send()
    for r in range(count - size, count):
        give_back(r)
    pltpu.make_async_copy(
        result.at[0, :, half(core)], out.at[me, core], own_sems.at[1]
    ).wait()
    for r in range(1, count):
        for c in range(2):
            remote(
                result.at[r, :, half(c)],
                out.at[peers[r], c],
                back_send.at[r, c],
                back_recv.at[r, c],
                {"gx": peers[r]},
            ).wait_recv()
    remote(
        result.at[0, :, half(core)],
        out.at[me, 1 - core],
        back_send.at[0, 0],
        back_recv.at[0, 1 - core],
        pair,
    ).wait_recv()
    for copy in backs:
        copy.wait_send()


def through_experts(values, up, down, collective_id):
    count = lax.axis_size("gx")
    slots, width = values.shape[1:]
    return pl.pallas_call(
        functools.partial(expert_kernel, count),
        out_shape=jax.ShapeDtypeStruct((count, 2, slots, width // 2), values.dtype),
        in_specs=[VMEM, VMEM, VMEM],
        out_specs=VMEM,
        scratch_shapes=[
            pltpu.VMEM(values.shape, values.dtype),
            pltpu.VMEM(values.shape, values.dtype),
            pltpu.VMEM(up.shape, up.dtype),
            pltpu.VMEM(down.shape, down.dtype),
            pltpu.SemaphoreType.DMA((count,)),
            pltpu.SemaphoreType.DMA((count,)),
            pltpu.SemaphoreType.DMA((count, 2)),
            pltpu.SemaphoreType.DMA((count, 2)),
            pltpu.SemaphoreType.DMA((2,)),
            pltpu.SemaphoreType.DMA((4,)),
            pltpu.SemaphoreType.DMA((count,)),
            pltpu.SemaphoreType.DMA((count,)),
        ],
        compiler_params=pltpu.CompilerParams(
            collective_id=collective_id, has_side_effects=True, vmem_limit_bytes=40 * 2**20
        ),
        cost_estimate=pl.CostEstimate(
            flops=0, bytes_accessed=200_000_000, transcendentals=0
        ),
    )(values, up, down)


def pair_kernel(src, out, send_sem, recv_sem, own_sem):
    lane = lax.axis_index("gy")
    core = lax.rem(lane, 2)
    pair = {"gy": lane + 1 - 2 * core}
    greet([pair])
    copy = remote(src.at[1 - core], out.at[core], send_sem, recv_sem, pair)
    copy.start()
    own = pltpu.make_async_copy(src.at[core], out.at[core], own_sem)
    own.start()
    own.wait()
    copy.wait_send()
    remote(src.at[core], out.at[1 - core], send_sem, recv_sem, pair).wait_recv()


def pair_swap(values, collective_id):
    return pl.pallas_call(
        pair_kernel,
        out_shape=jax.ShapeDtypeStruct(values.shape, values.dtype),
        in_specs=[VMEM],
        out_specs=VMEM,
        scratch_shapes=[pltpu.SemaphoreType.DMA] * 3,
        compiler_params=pltpu.CompilerParams(collective_id=collective_id, has_side_effects=True),
    )(values)


def relay_kernel(count, *refs):
    src, out, send_sem, recv_sem, own_sem = refs
    me = lax.axis_index("gx")
    y_chips = count // X_CHIPS
    y, x = me // X_CHIPS, lax.rem(me, X_CHIPS)

    def at(row, column):
        return lax.rem(row + y_chips, y_chips) * X_CHIPS + lax.rem(column, X_CHIPS)

    above, below = at(y + 1, x), at(y - 1, x)
    right, left = at(y, x + 1), at(y, x + 3)
    greet([{"gx": other} for other in (above, below, right, left)])
    sent = []

    def send(block, source, target):
        copy = remote(
            source, out.at[block], send_sem.at[len(sent)], recv_sem.at[block], {"gx": target}
        )
        copy.start()
        sent.append(copy)

    def arrived(block):
        remote(
            src, out.at[block], send_sem.at[0], recv_sem.at[block], {"gx": above}
        ).wait_recv()

    def across(k):
        near, far = (x + 3, right) if k % 2 == 0 else (x + 1, left)
        block = at(y + k, near)
        arrived(block)
        send(block, out.at[block], far)

    send(me, src, above)
    send(me, src, below)
    send(me, src, right)
    send(me, src, left)
    own = pltpu.make_async_copy(src, out.at[me], own_sem)
    own.start()
    half = y_chips // 2
    order = [0]
    for step in range(1, half + 1):
        order.append(y_chips - step)
        if step < half:
            order.append(step)
    for i, k in enumerate(order):
        if k:
            block = at(y + k, x)
            arrived(block)
            if half < k:
                send(block, out.at[block], above)
            elif k < half - 1:
                send(block, out.at[block], below)
            send(block, out.at[block], right)
            send(block, out.at[block], left)
        if i >= 1:
            across(order[i - 1])
    across(order[-1])
    for k in order:
        arrived(at(y + k, x + (1 if k % 2 == 0 else 3)))
        arrived(at(y + k, x + 2))
    own.wait()
    for copy in sent:
        copy.wait_send()


def relay_gather(values, collective_id):
    count = lax.axis_size("gx")
    return pl.pallas_call(
        functools.partial(relay_kernel, count),
        out_shape=jax.ShapeDtypeStruct((count,) + values.shape, values.dtype),
        in_specs=[VMEM],
        out_specs=VMEM,
        scratch_shapes=[
            pltpu.SemaphoreType.DMA((count,)),
            pltpu.SemaphoreType.DMA((count,)),
            pltpu.SemaphoreType.DMA,
        ],
        compiler_params=pltpu.CompilerParams(collective_id=collective_id, has_side_effects=True),
        cost_estimate=pl.CostEstimate(
            flops=0, bytes_accessed=40_000_000, transcendentals=0
        ),
    )(values)


def shards(
    hidden_in, norm_gain, router_weight, routes, w_gate_up, w_down, final_gain, head_weight, targets
):
    tok_rows = hidden_in.shape[0]
    width = hidden_in.shape[1]
    group_count = lax.axis_size("gx")
    lane_count = lax.axis_size("gy")
    group_index = lax.axis_index("gx")
    lane_index = lax.axis_index("gy")
    expert_count = router_weight.shape[1]
    slot_count = tok_rows // 8
    half_slots = slot_count // 2
    share_rows = tok_rows // lane_count
    columns = head_weight.shape[1]
    head_full = lax.all_gather(head_weight, "gy", axis=0, tiled=True)
    normed = rms_scale(hidden_in, norm_gain).astype(jnp.bfloat16)
    scores = jnp.dot(normed, router_weight, preferred_element_type=jnp.float32)
    chosen = routes[:, :, None] == jnp.arange(expert_count, dtype=jnp.int32)[None, None, :]
    picked = jnp.sum(jnp.where(chosen, scores[:, None, :], 0.0), -1)
    gate_values = jax.nn.softmax(picked, axis=-1).astype(jnp.bfloat16)
    gate_table = jnp.sum(jnp.where(chosen, gate_values.astype(jnp.float32)[:, :, None], 0.0), 1)
    member = jnp.sum(chosen.astype(jnp.int32), 1)
    slot_rank = jnp.cumsum(member, 0) - member
    slot_hit = (member[:, :, None] == 1) & (
        slot_rank[:, :, None] == jnp.arange(slot_count, dtype=jnp.int32)[None, None, :]
    )
    owner_expert = (
        jnp.arange(group_count, dtype=jnp.int32) * lane_count + lane_index
    ) // SPLITS
    pick_expert = (
        owner_expert[:, None] == jnp.arange(expert_count, dtype=jnp.int32)[None, :]
    ).astype(jnp.bfloat16)
    dispatch = jnp.einsum(
        "te,nec->tcn",
        pick_expert,
        slot_hit.astype(jnp.bfloat16),
        preferred_element_type=jnp.float32,
    ).astype(jnp.bfloat16)
    core = lax.rem(lane_index, 2)
    own_slots = lax.dynamic_slice_in_dim(dispatch, core * half_slots, half_slots, 1)
    outgoing = jnp.einsum(
        "tcn,nd->tcd", own_slots, normed, preferred_element_type=jnp.float32
    ).astype(jnp.bfloat16)
    expert_gate = jnp.einsum(
        "te,ne->tn",
        pick_expert,
        gate_table.astype(jnp.bfloat16),
        preferred_element_type=jnp.float32,
    )
    combine = (dispatch.astype(jnp.float32) * expert_gate[:, None, :]).astype(jnp.bfloat16)
    returned = through_experts(outgoing, w_gate_up[0], w_down[0], 1)
    partial_value = jnp.einsum(
        "tcn,tcd->nd",
        combine,
        returned.reshape(group_count, slot_count, width // 2),
        preferred_element_type=jnp.float32,
    ).astype(jnp.bfloat16)
    chips = lane_count // 2
    pieces = exchange(partial_value.reshape(chips, 2 * share_rows, width // 2), "gy", 3)
    halves = pair_swap(
        jnp.sum(pieces.astype(jnp.float32), 0).reshape(2, share_rows, width // 2), 6
    )
    summed = jnp.concatenate([halves[0], halves[1]], axis=-1)
    residual = lax.dynamic_slice_in_dim(hidden_in, lane_index * share_rows, share_rows, 0)
    layer_out = (residual.astype(jnp.float32) + summed).astype(jnp.bfloat16)
    final_states = rms_scale(layer_out, final_gain).astype(jnp.bfloat16)
    gathered = relay_gather(final_states, 4).reshape(group_count * share_rows, width)
    target_grid = targets.reshape(group_count, tok_rows)
    logits = jnp.dot(gathered, head_full, preferred_element_type=jnp.float32)
    offset = group_index * columns
    own_targets = lax.dynamic_slice_in_dim(
        target_grid, lane_index * share_rows, share_rows, 1
    ).reshape(group_count * share_rows)
    target_hits = (offset + jnp.arange(columns, dtype=jnp.int32))[None, :] == own_targets[:, None]
    local_peak = jnp.max(logits, -1)
    shifted = logits - local_peak[:, None]
    weights = jnp.exp(shifted)
    local = jnp.stack(
        [
            local_peak,
            jnp.sum(weights, -1),
            jnp.sum(weights * shifted, -1),
            jnp.sum(jnp.where(target_hits, logits, 0.0), -1),
        ]
    )
    stats = exchange(local, "gx", 5, same=True)
    peaks, masses, spreads = stats[:, 0], stats[:, 1], stats[:, 2]
    peak_value = jnp.max(peaks, 0)
    below = peaks - peak_value[None, :]
    scale = jnp.exp(below)
    total_mass = jnp.sum(masses * scale, 0)
    spread = jnp.sum(scale * (spreads + below * masses), 0)
    log_mass = jnp.log(total_mass)
    logprob = jnp.sum(stats[:, 3], 0) - peak_value - log_mass
    entropy = log_mass - spread / total_mass
    return (logprob.reshape(group_count, share_rows), entropy.reshape(group_count, share_rows))


def solution(mesh):
    return jax.shard_map(
        shards,
        mesh=mesh,
        in_specs=(
            P("gx", None),
            P(),
            P(),
            P("gx", None),
            P(("gx", "gy"), None, None),
            P(("gx", "gy"), None, None),
            P(),
            P("gy", "gx"),
            P(),
        ),
        out_specs=(P(None, "gy"), P(None, "gy")),
        check_vma=False,
    )
```

```python
import functools

import jax
import jax.numpy as jnp
from jax import lax
from jax.experimental import pallas as pl
from jax.experimental.pallas import tpu as pltpu
from jax.sharding import PartitionSpec as P

SPLITS = 8
X_CHIPS = 4

NORM_EPSILON = 1e-06

VMEM = pl.BlockSpec(memory_space=pltpu.VMEM)


def rms_scale(values, gain_vector):
    widened = values.astype(jnp.float32)
    return (
        widened
        * lax.rsqrt(jnp.mean(widened * widened, -1, keepdims=True) + NORM_EPSILON)
        * gain_vector.astype(jnp.float32)
    )


def remote(src, dst, send_sem, recv_sem, device):
    return pltpu.make_async_remote_copy(
        src_ref=src,
        dst_ref=dst,
        send_sem=send_sem,
        recv_sem=recv_sem,
        device_id=device,
        device_id_type=pl.DeviceIdType.MESH,
    )


def greet(devices):
    barrier = pltpu.get_barrier_semaphore()
    for device in devices:
        pl.semaphore_signal(
            barrier, inc=1, device_id=device, device_id_type=pl.DeviceIdType.MESH
        )
    pl.semaphore_wait(barrier, len(devices))


def offsets(axis, count):
    if axis == "gy":
        steps = []
        for z in range(1, count // 2 + 1):
            steps += [z] if 2 * z == count else [z, -z]
        return steps
    y_chips = count // X_CHIPS
    steps = []
    for y in range(0, y_chips // 2 + 1):
        for x in range(X_CHIPS):
            for sign in (1, -1):
                if (y == 0 or 2 * y == y_chips) and sign == -1:
                    continue
                if y or x:
                    steps.append((sign * y, x))
    return steps


def partners(axis, count, me):
    if axis == "gy":
        return [lax.rem(me + step + count, count) for step in offsets(axis, count)]
    y_chips = count // X_CHIPS
    y, x = me // X_CHIPS, lax.rem(me, X_CHIPS)
    return [
        lax.rem(y + dy + y_chips, y_chips) * X_CHIPS + lax.rem(x + dx, X_CHIPS)
        for dy, dx in offsets(axis, count)
    ]


def exchange_kernel(axis, same, count, *refs):
    src, out, send_sem, recv_sem, own_sem = refs
    me = lax.axis_index(axis)
    core = 0
    if axis == "gy":
        me, core = me // 2, lax.rem(me, 2)

    def device(other):
        return {axis: 2 * other + core if axis == "gy" else other}

    others = partners(axis, count, me)
    greet([device(other) for other in others])
    copies = [
        remote(
            src if same else src.at[other],
            out.at[me],
            send_sem.at[other],
            recv_sem.at[me],
            device(other),
        )
        for other in others
    ]
    for copy in copies:
        copy.start()
    own = pltpu.make_async_copy(src if same else src.at[me], out.at[me], own_sem)
    own.start()
    own.wait()
    for other in others:
        remote(
            src if same else src.at[other],
            out.at[other],
            send_sem.at[other],
            recv_sem.at[other],
            device(other),
        ).wait_recv()
    for copy in copies:
        copy.wait_send()


def exchange(values, axis, collective_id, same=False):
    count = lax.axis_size(axis) // (2 if axis == "gy" else 1)
    shape = (count,) + values.shape if same else values.shape
    return pl.pallas_call(
        functools.partial(exchange_kernel, axis, same, count),
        out_shape=jax.ShapeDtypeStruct(shape, values.dtype),
        in_specs=[VMEM],
        out_specs=VMEM,
        scratch_shapes=[
            pltpu.SemaphoreType.DMA((count,)),
            pltpu.SemaphoreType.DMA((count,)),
            pltpu.SemaphoreType.DMA,
        ],
        compiler_params=pltpu.CompilerParams(collective_id=collective_id, has_side_effects=True),
        cost_estimate=pl.CostEstimate(
            flops=0, bytes_accessed=40_000_000, transcendentals=0
        ),
    )(values)


def expert_kernel(count, *refs):
    (src, up, down, out, rows, result, other_up, other_down) = refs[:8]
    (send_sem, recv_sem, back_send, back_recv, own_sems, pair_sems) = refs[8:14]
    (hand_send, hand_recv) = refs[14:]
    me = lax.axis_index("gx")
    lane = lax.axis_index("gy")
    core = lax.rem(lane, 2)
    first = lane - core
    pair = {"gy": first + 1 - core}
    side = lax.rem(lane // 2, 2)
    next_chip = {"gy": lane + 2 - 4 * side}
    slots, width = src.shape[1:]
    wide = width // 2
    units = down.shape[0]
    y_chips = count // X_CHIPS
    steps = [(0, 0)] + [(dy % y_chips, dx) for dy, dx in offsets("gx", count)]
    y, x = me // X_CHIPS, lax.rem(me, X_CHIPS)
    peers = [
        lax.rem(y + dy, y_chips) * X_CHIPS + lax.rem(x + dx, X_CHIPS) for dy, dx in steps
    ]
    mirror = [
        steps.index(((y_chips - dy) % y_chips, (X_CHIPS - dx) % X_CHIPS)) for dy, dx in steps
    ]
    greet(
        [pair, next_chip]
        + [{"gx": other, "gy": first + c} for other in peers[1:] for c in range(2)]
    )

    def half(c):
        return pl.ds(pl.multiple_of(c * wide, 128), wide)

    swaps = [
        remote(up, other_up, pair_sems.at[0], pair_sems.at[1], pair),
        remote(down, other_down, pair_sems.at[2], pair_sems.at[3], pair),
    ]
    for copy in swaps:
        copy.start()
    sent = [
        remote(
            src.at[peers[r], :, half(side)],
            rows.at[mirror[r], :, half(side)],
            send_sem.at[r],
            recv_sem.at[mirror[r]],
            {"gx": peers[r]},
        )
        for r in range(1, count)
    ]
    for copy in sent:
        copy.start()
    own = pltpu.make_async_copy(src.at[me], rows.at[0], own_sems.at[0])
    own.start()
    own.wait()
    backs = []

    def give_back(r):
        for c in range(2):
            if r:
                copy = remote(
                    result.at[r, :, half(c)],
                    out.at[me, core],
                    back_send.at[r, c],
                    back_recv.at[mirror[r], core],
                    {"gx": peers[r], "gy": first + c},
                )
                copy.start()
                backs.append(copy)
        if not r:
            copy = remote(
                result.at[0, :, half(1 - core)],
                out.at[me, core],
                back_send.at[0, 0],
                back_recv.at[0, core],
                pair,
            )
            copy.start()
            backs.append(copy)
            pltpu.make_async_copy(
                result.at[0, :, half(core)], out.at[me, core], own_sems.at[1]
            ).start()

    def block(chunk, up_ref, down_ref):
        lifted = jnp.dot(chunk, up_ref[...], preferred_element_type=jnp.float32)
        gate = lifted[:, :units]
        active = gate / (1.0 + jnp.exp(-gate)) * lifted[:, units:]
        return jnp.dot(
            active.astype(jnp.bfloat16), down_ref[...], preferred_element_type=jnp.float32
        )

    size = 8
    hands = []

    def hand_on(base):
        for r in range(max(base, 1), base + size):
            remote(
                src.at[peers[r], :, half(side)],
                rows.at[r, :, half(side)],
                send_sem.at[r],
                recv_sem.at[r],
                {"gx": peers[r]},
            ).wait_recv()
            hand = remote(
                rows.at[r, :, half(side)],
                rows.at[r, :, half(side)],
                hand_send.at[r],
                hand_recv.at[r],
                next_chip,
            )
            hand.start()
            hands.append(hand)

    hand_on(0)
    for copy in swaps:
        copy.wait_recv()
    for base in range(0, count, size):
        if base + size < count:
            hand_on(base + size)
        if base:
            for r in range(base - size, base):
                give_back(r)
        for r in range(max(base, 1), base + size):
            remote(
                rows.at[r, :, half(side)],
                rows.at[r, :, half(1 - side)],
                hand_send.at[r],
                hand_recv.at[r],
                next_chip,
            ).wait_recv()
        chunk = rows[pl.ds(base, size)].reshape(size * slots, width)
        total = block(chunk, up, down) + block(chunk, other_up, other_down)
        result[pl.ds(base, size)] = total.astype(jnp.bfloat16).reshape(size, slots, width)
    for copy in sent + swaps + hands:
        copy.wait_send()
    for r in range(count - size, count):
        give_back(r)
    pltpu.make_async_copy(
        result.at[0, :, half(core)], out.at[me, core], own_sems.at[1]
    ).wait()
    for r in range(1, count):
        for c in range(2):
            remote(
                result.at[r, :, half(c)],
                out.at[peers[r], c],
                back_send.at[r, c],
                back_recv.at[r, c],
                {"gx": peers[r]},
            ).wait_recv()
    remote(
        result.at[0, :, half(core)],
        out.at[me, 1 - core],
        back_send.at[0, 0],
        back_recv.at[0, 1 - core],
        pair,
    ).wait_recv()
    for copy in backs:
        copy.wait_send()


def through_experts(values, up, down, collective_id):
    count = lax.axis_size("gx")
    slots, width = values.shape[1:]
    return pl.pallas_call(
        functools.partial(expert_kernel, count),
        out_shape=jax.ShapeDtypeStruct((count, 2, slots, width // 2), values.dtype),
        in_specs=[VMEM, VMEM, VMEM],
        out_specs=VMEM,
        scratch_shapes=[
            pltpu.VMEM(values.shape, values.dtype),
            pltpu.VMEM(values.shape, values.dtype),
            pltpu.VMEM(up.shape, up.dtype),
            pltpu.VMEM(down.shape, down.dtype),
            pltpu.SemaphoreType.DMA((count,)),
            pltpu.SemaphoreType.DMA((count,)),
            pltpu.SemaphoreType.DMA((count, 2)),
            pltpu.SemaphoreType.DMA((count, 2)),
            pltpu.SemaphoreType.DMA((2,)),
            pltpu.SemaphoreType.DMA((4,)),
            pltpu.SemaphoreType.DMA((count,)),
            pltpu.SemaphoreType.DMA((count,)),
        ],
        compiler_params=pltpu.CompilerParams(
            collective_id=collective_id, has_side_effects=True, vmem_limit_bytes=40 * 2**20
        ),
        cost_estimate=pl.CostEstimate(
            flops=0, bytes_accessed=200_000_000, transcendentals=0
        ),
    )(values, up, down)


def pair_kernel(src, out, send_sem, recv_sem, own_sem):
    lane = lax.axis_index("gy")
    core = lax.rem(lane, 2)
    pair = {"gy": lane + 1 - 2 * core}
    greet([pair])
    copy = remote(src.at[1 - core], out.at[core], send_sem, recv_sem, pair)
    copy.start()
    own = pltpu.make_async_copy(src.at[core], out.at[core], own_sem)
    own.start()
    own.wait()
    copy.wait_send()
    remote(src.at[core], out.at[1 - core], send_sem, recv_sem, pair).wait_recv()


def pair_swap(values, collective_id):
    return pl.pallas_call(
        pair_kernel,
        out_shape=jax.ShapeDtypeStruct(values.shape, values.dtype),
        in_specs=[VMEM],
        out_specs=VMEM,
        scratch_shapes=[pltpu.SemaphoreType.DMA] * 3,
        compiler_params=pltpu.CompilerParams(collective_id=collective_id, has_side_effects=True),
    )(values)


def relay_kernel(count, *refs):
    src, out, send_sem, recv_sem, own_sem = refs
    me = lax.axis_index("gx")
    y_chips = count // X_CHIPS
    y, x = me // X_CHIPS, lax.rem(me, X_CHIPS)

    def at(row, column):
        return lax.rem(row + y_chips, y_chips) * X_CHIPS + lax.rem(column, X_CHIPS)

    above, below = at(y + 1, x), at(y - 1, x)
    above2, below2 = at(y + 2, x), at(y - 2, x)
    right, left = at(y, x + 1), at(y, x + 3)
    greet([{"gx": other} for other in (above, below, above2, below2, right, left)])
    sent = []

    def send(block, source, target):
        copy = remote(
            source, out.at[block], send_sem.at[len(sent)], recv_sem.at[block], {"gx": target}
        )
        copy.start()
        sent.append(copy)

    def arrived(block):
        remote(
            src, out.at[block], send_sem.at[0], recv_sem.at[block], {"gx": above}
        ).wait_recv()

    def across(k):
        near, far = (x + 3, right) if k % 2 == 0 else (x + 1, left)
        block = at(y + k, near)
        arrived(block)
        send(block, out.at[block], far)

    send(me, src, above)
    send(me, src, below)
    send(me, src, above2)
    send(me, src, below2)
    send(me, src, right)
    send(me, src, left)
    own = pltpu.make_async_copy(src, out.at[me], own_sem)
    own.start()
    assert y_chips == 8
    half = y_chips // 2
    order = [0]
    for step in range(1, half + 1):
        order.append(y_chips - step)
        if step < half:
            order.append(step)
    for i, k in enumerate(order):
        if k:
            block = at(y + k, x)
            arrived(block)
            if k == y_chips - 2:
                send(block, out.at[block], above2)
                send(block, out.at[block], above)
            elif k == 2:
                send(block, out.at[block], below)
            send(block, out.at[block], right)
            send(block, out.at[block], left)
        if i >= 1:
            across(order[i - 1])
    across(order[-1])
    for k in order:
        arrived(at(y + k, x + (1 if k % 2 == 0 else 3)))
        arrived(at(y + k, x + 2))
    own.wait()
    for copy in sent:
        copy.wait_send()


def relay_gather(values, collective_id):
    count = lax.axis_size("gx")
    return pl.pallas_call(
        functools.partial(relay_kernel, count),
        out_shape=jax.ShapeDtypeStruct((count,) + values.shape, values.dtype),
        in_specs=[VMEM],
        out_specs=VMEM,
        scratch_shapes=[
            pltpu.SemaphoreType.DMA((count,)),
            pltpu.SemaphoreType.DMA((count,)),
            pltpu.SemaphoreType.DMA,
        ],
        compiler_params=pltpu.CompilerParams(collective_id=collective_id, has_side_effects=True),
        cost_estimate=pl.CostEstimate(
            flops=0, bytes_accessed=40_000_000, transcendentals=0
        ),
    )(values)


def shards(
    hidden_in, norm_gain, router_weight, routes, w_gate_up, w_down, final_gain, head_weight, targets
):
    tok_rows = hidden_in.shape[0]
    width = hidden_in.shape[1]
    group_count = lax.axis_size("gx")
    lane_count = lax.axis_size("gy")
    group_index = lax.axis_index("gx")
    lane_index = lax.axis_index("gy")
    expert_count = router_weight.shape[1]
    slot_count = tok_rows // 8
    half_slots = slot_count // 2
    share_rows = tok_rows // lane_count
    columns = head_weight.shape[1]
    head_full = lax.all_gather(head_weight, "gy", axis=0, tiled=True)
    normed = rms_scale(hidden_in, norm_gain).astype(jnp.bfloat16)
    scores = jnp.dot(normed, router_weight, preferred_element_type=jnp.float32)
    chosen = routes[:, :, None] == jnp.arange(expert_count, dtype=jnp.int32)[None, None, :]
    picked = jnp.sum(jnp.where(chosen, scores[:, None, :], 0.0), -1)
    gate_values = jax.nn.softmax(picked, axis=-1).astype(jnp.bfloat16)
    gate_table = jnp.sum(jnp.where(chosen, gate_values.astype(jnp.float32)[:, :, None], 0.0), 1)
    member = jnp.sum(chosen.astype(jnp.int32), 1)
    slot_rank = jnp.cumsum(member, 0) - member
    slot_hit = (member[:, :, None] == 1) & (
        slot_rank[:, :, None] == jnp.arange(slot_count, dtype=jnp.int32)[None, None, :]
    )
    owner_expert = (
        jnp.arange(group_count, dtype=jnp.int32) * lane_count + lane_index
    ) // SPLITS
    pick_expert = (
        owner_expert[:, None] == jnp.arange(expert_count, dtype=jnp.int32)[None, :]
    ).astype(jnp.bfloat16)
    dispatch = jnp.einsum(
        "te,nec->tcn",
        pick_expert,
        slot_hit.astype(jnp.bfloat16),
        preferred_element_type=jnp.float32,
    ).astype(jnp.bfloat16)
    core = lax.rem(lane_index, 2)
    own_slots = lax.dynamic_slice_in_dim(dispatch, core * half_slots, half_slots, 1)
    outgoing = jnp.einsum(
        "tcn,nd->tcd", own_slots, normed, preferred_element_type=jnp.float32
    ).astype(jnp.bfloat16)
    expert_gate = jnp.einsum(
        "te,ne->tn",
        pick_expert,
        gate_table.astype(jnp.bfloat16),
        preferred_element_type=jnp.float32,
    )
    combine = (dispatch.astype(jnp.float32) * expert_gate[:, None, :]).astype(jnp.bfloat16)
    returned = through_experts(outgoing, w_gate_up[0], w_down[0], 1)
    partial_value = jnp.einsum(
        "tcn,tcd->nd",
        combine,
        returned.reshape(group_count, slot_count, width // 2),
        preferred_element_type=jnp.float32,
    ).astype(jnp.bfloat16)
    chips = lane_count // 2
    pieces = exchange(partial_value.reshape(chips, 2 * share_rows, width // 2), "gy", 3)
    halves = pair_swap(
        jnp.sum(pieces.astype(jnp.float32), 0).reshape(2, share_rows, width // 2), 6
    )
    summed = jnp.concatenate([halves[0], halves[1]], axis=-1)
    residual = lax.dynamic_slice_in_dim(hidden_in, lane_index * share_rows, share_rows, 0)
    layer_out = (residual.astype(jnp.float32) + summed).astype(jnp.bfloat16)
    final_states = rms_scale(layer_out, final_gain).astype(jnp.bfloat16)
    gathered = relay_gather(final_states, 4).reshape(group_count * share_rows, width)
    target_grid = targets.reshape(group_count, tok_rows)
    logits = jnp.dot(gathered, head_full, preferred_element_type=jnp.float32)
    offset = group_index * columns
    own_targets = lax.dynamic_slice_in_dim(
        target_grid, lane_index * share_rows, share_rows, 1
    ).reshape(group_count * share_rows)
    target_hits = (offset + jnp.arange(columns, dtype=jnp.int32))[None, :] == own_targets[:, None]
    local_peak = jnp.max(logits, -1)
    shifted = logits - local_peak[:, None]
    weights = jnp.exp(shifted)
    local = jnp.stack(
        [
            local_peak,
            jnp.sum(weights, -1),
            jnp.sum(weights * shifted, -1),
            jnp.sum(jnp.where(target_hits, logits, 0.0), -1),
        ]
    )
    stats = exchange(local, "gx", 5, same=True)
    peaks, masses, spreads = stats[:, 0], stats[:, 1], stats[:, 2]
    peak_value = jnp.max(peaks, 0)
    below = peaks - peak_value[None, :]
    scale = jnp.exp(below)
    total_mass = jnp.sum(masses * scale, 0)
    spread = jnp.sum(scale * (spreads + below * masses), 0)
    log_mass = jnp.log(total_mass)
    logprob = jnp.sum(stats[:, 3], 0) - peak_value - log_mass
    entropy = log_mass - spread / total_mass
    return (logprob.reshape(group_count, share_rows), entropy.reshape(group_count, share_rows))


def solution(mesh):
    return jax.shard_map(
        shards,
        mesh=mesh,
        in_specs=(
            P("gx", None),
            P(),
            P(),
            P("gx", None),
            P(("gx", "gy"), None, None),
            P(("gx", "gy"), None, None),
            P(),
            P("gy", "gx"),
            P(),
        ),
        out_specs=(P(None, "gy"), P(None, "gy")),
        check_vma=False,
    )
```

```python
import functools

import jax
import jax.numpy as jnp
from jax import lax
from jax.experimental import pallas as pl
from jax.experimental.pallas import tpu as pltpu
from jax.sharding import PartitionSpec as P

SPLITS = 8
X_CHIPS = 4

NORM_EPSILON = 1e-06

VMEM = pl.BlockSpec(memory_space=pltpu.VMEM)


def rms_scale(values, gain_vector):
    widened = values.astype(jnp.float32)
    return (
        widened
        * lax.rsqrt(jnp.mean(widened * widened, -1, keepdims=True) + NORM_EPSILON)
        * gain_vector.astype(jnp.float32)
    )


def remote(src, dst, send_sem, recv_sem, device):
    return pltpu.make_async_remote_copy(
        src_ref=src,
        dst_ref=dst,
        send_sem=send_sem,
        recv_sem=recv_sem,
        device_id=device,
        device_id_type=pl.DeviceIdType.MESH,
    )


def greet(devices):
    barrier = pltpu.get_barrier_semaphore()
    for device in devices:
        pl.semaphore_signal(
            barrier, inc=1, device_id=device, device_id_type=pl.DeviceIdType.MESH
        )
    pl.semaphore_wait(barrier, len(devices))


def offsets(axis, count):
    if axis == "gy":
        steps = []
        for z in range(1, count // 2 + 1):
            steps += [z] if 2 * z == count else [z, -z]
        return steps
    y_chips = count // X_CHIPS
    steps = []
    for y in range(0, y_chips // 2 + 1):
        for x in range(X_CHIPS):
            for sign in (1, -1):
                if (y == 0 or 2 * y == y_chips) and sign == -1:
                    continue
                if y or x:
                    steps.append((sign * y, x))
    return steps


def partners(axis, count, me):
    if axis == "gy":
        return [lax.rem(me + step + count, count) for step in offsets(axis, count)]
    y_chips = count // X_CHIPS
    y, x = me // X_CHIPS, lax.rem(me, X_CHIPS)
    return [
        lax.rem(y + dy + y_chips, y_chips) * X_CHIPS + lax.rem(x + dx, X_CHIPS)
        for dy, dx in offsets(axis, count)
    ]


def exchange_kernel(axis, same, count, *refs):
    src, out, send_sem, recv_sem, own_sem = refs
    me = lax.axis_index(axis)
    core = 0
    if axis == "gy":
        me, core = me // 2, lax.rem(me, 2)

    def device(other):
        return {axis: 2 * other + core if axis == "gy" else other}

    others = partners(axis, count, me)
    greet([device(other) for other in others])
    copies = [
        remote(
            src if same else src.at[other],
            out.at[me],
            send_sem.at[other],
            recv_sem.at[me],
            device(other),
        )
        for other in others
    ]
    for copy in copies:
        copy.start()
    own = pltpu.make_async_copy(src if same else src.at[me], out.at[me], own_sem)
    own.start()
    own.wait()
    for other in others:
        remote(
            src if same else src.at[other],
            out.at[other],
            send_sem.at[other],
            recv_sem.at[other],
            device(other),
        ).wait_recv()
    for copy in copies:
        copy.wait_send()


def exchange(values, axis, collective_id, same=False):
    count = lax.axis_size(axis) // (2 if axis == "gy" else 1)
    shape = (count,) + values.shape if same else values.shape
    return pl.pallas_call(
        functools.partial(exchange_kernel, axis, same, count),
        out_shape=jax.ShapeDtypeStruct(shape, values.dtype),
        in_specs=[VMEM],
        out_specs=VMEM,
        scratch_shapes=[
            pltpu.SemaphoreType.DMA((count,)),
            pltpu.SemaphoreType.DMA((count,)),
            pltpu.SemaphoreType.DMA,
        ],
        compiler_params=pltpu.CompilerParams(collective_id=collective_id, has_side_effects=True),
        cost_estimate=pl.CostEstimate(
            flops=0, bytes_accessed=40_000_000, transcendentals=0
        ),
    )(values)


def expert_kernel(count, *refs):
    (src, up, down, out, rows, result, other_up, other_down) = refs[:8]
    (send_sem, recv_sem, back_send, back_recv, own_sems, pair_sems) = refs[8:14]
    (hand_send, hand_recv) = refs[14:]
    me = lax.axis_index("gx")
    lane = lax.axis_index("gy")
    core = lax.rem(lane, 2)
    first = lane - core
    pair = {"gy": first + 1 - core}
    side = lax.rem(lane // 2, 2)
    next_chip = {"gy": lane + 2 - 4 * side}
    slots, width = src.shape[1:]
    wide = width // 2
    units = down.shape[0]
    y_chips = count // X_CHIPS
    steps = [(0, 0)] + [(dy % y_chips, dx) for dy, dx in offsets("gx", count)]
    y, x = me // X_CHIPS, lax.rem(me, X_CHIPS)
    peers = [
        lax.rem(y + dy, y_chips) * X_CHIPS + lax.rem(x + dx, X_CHIPS) for dy, dx in steps
    ]
    mirror = [
        steps.index(((y_chips - dy) % y_chips, (X_CHIPS - dx) % X_CHIPS)) for dy, dx in steps
    ]
    greet(
        [pair, next_chip]
        + [{"gx": other, "gy": first + c} for other in peers[1:] for c in range(2)]
    )

    def half(c):
        return pl.ds(pl.multiple_of(c * wide, 128), wide)

    swaps = [
        remote(up, other_up, pair_sems.at[0], pair_sems.at[1], pair),
        remote(down, other_down, pair_sems.at[2], pair_sems.at[3], pair),
    ]
    for copy in swaps:
        copy.start()
    sent = [
        remote(
            src.at[peers[r], :, half(side)],
            rows.at[mirror[r], :, half(side)],
            send_sem.at[r],
            recv_sem.at[mirror[r]],
            {"gx": peers[r]},
        )
        for r in range(1, count)
    ]
    for copy in sent:
        copy.start()
    own = pltpu.make_async_copy(src.at[me], rows.at[0], own_sems.at[0])
    own.start()
    own.wait()
    backs = []

    def give_back(r):
        for c in range(2):
            if r:
                copy = remote(
                    result.at[r, :, half(c)],
                    out.at[me, core],
                    back_send.at[r, c],
                    back_recv.at[mirror[r], core],
                    {"gx": peers[r], "gy": first + c},
                )
                copy.start()
                backs.append(copy)
        if not r:
            copy = remote(
                result.at[0, :, half(1 - core)],
                out.at[me, core],
                back_send.at[0, 0],
                back_recv.at[0, core],
                pair,
            )
            copy.start()
            backs.append(copy)
            pltpu.make_async_copy(
                result.at[0, :, half(core)], out.at[me, core], own_sems.at[1]
            ).start()

    def block(chunk, up_ref, down_ref):
        lifted = jnp.dot(chunk, up_ref[...], preferred_element_type=jnp.float32)
        gate = lifted[:, :units]
        active = gate / (1.0 + jnp.exp(-gate)) * lifted[:, units:]
        return jnp.dot(
            active.astype(jnp.bfloat16), down_ref[...], preferred_element_type=jnp.float32
        )

    size = 8
    hands = []

    def hand_on(base):
        for r in range(max(base, 1), base + size):
            remote(
                src.at[peers[r], :, half(side)],
                rows.at[r, :, half(side)],
                send_sem.at[r],
                recv_sem.at[r],
                {"gx": peers[r]},
            ).wait_recv()
            hand = remote(
                rows.at[r, :, half(side)],
                rows.at[r, :, half(side)],
                hand_send.at[r],
                hand_recv.at[r],
                next_chip,
            )
            hand.start()
            hands.append(hand)

    hand_on(0)
    for copy in swaps:
        copy.wait_recv()
    for base in range(0, count, size):
        if base + size < count:
            hand_on(base + size)
        if base:
            for r in range(base - size, base):
                give_back(r)
        for r in range(max(base, 1), base + size):
            remote(
                rows.at[r, :, half(side)],
                rows.at[r, :, half(1 - side)],
                hand_send.at[r],
                hand_recv.at[r],
                next_chip,
            ).wait_recv()
        chunk = rows[pl.ds(base, size)].reshape(size * slots, width)
        total = block(chunk, up, down) + block(chunk, other_up, other_down)
        result[pl.ds(base, size)] = total.astype(jnp.bfloat16).reshape(size, slots, width)
    for copy in sent + swaps + hands:
        copy.wait_send()
    for r in range(count - size, count):
        give_back(r)
    pltpu.make_async_copy(
        result.at[0, :, half(core)], out.at[me, core], own_sems.at[1]
    ).wait()
    for r in range(1, count):
        for c in range(2):
            remote(
                result.at[r, :, half(c)],
                out.at[peers[r], c],
                back_send.at[r, c],
                back_recv.at[r, c],
                {"gx": peers[r]},
            ).wait_recv()
    remote(
        result.at[0, :, half(core)],
        out.at[me, 1 - core],
        back_send.at[0, 0],
        back_recv.at[0, 1 - core],
        pair,
    ).wait_recv()
    for copy in backs:
        copy.wait_send()


def through_experts(values, up, down, collective_id):
    count = lax.axis_size("gx")
    slots, width = values.shape[1:]
    return pl.pallas_call(
        functools.partial(expert_kernel, count),
        out_shape=jax.ShapeDtypeStruct((count, 2, slots, width // 2), values.dtype),
        in_specs=[VMEM, VMEM, VMEM],
        out_specs=VMEM,
        scratch_shapes=[
            pltpu.VMEM(values.shape, values.dtype),
            pltpu.VMEM(values.shape, values.dtype),
            pltpu.VMEM(up.shape, up.dtype),
            pltpu.VMEM(down.shape, down.dtype),
            pltpu.SemaphoreType.DMA((count,)),
            pltpu.SemaphoreType.DMA((count,)),
            pltpu.SemaphoreType.DMA((count, 2)),
            pltpu.SemaphoreType.DMA((count, 2)),
            pltpu.SemaphoreType.DMA((2,)),
            pltpu.SemaphoreType.DMA((4,)),
            pltpu.SemaphoreType.DMA((count,)),
            pltpu.SemaphoreType.DMA((count,)),
        ],
        compiler_params=pltpu.CompilerParams(
            collective_id=collective_id, has_side_effects=True, vmem_limit_bytes=40 * 2**20
        ),
        cost_estimate=pl.CostEstimate(
            flops=0, bytes_accessed=200_000_000, transcendentals=0
        ),
    )(values, up, down)


def pair_kernel(src, out, send_sem, recv_sem, own_sem):
    lane = lax.axis_index("gy")
    core = lax.rem(lane, 2)
    pair = {"gy": lane + 1 - 2 * core}
    greet([pair])
    copy = remote(src.at[1 - core], out.at[core], send_sem, recv_sem, pair)
    copy.start()
    own = pltpu.make_async_copy(src.at[core], out.at[core], own_sem)
    own.start()
    own.wait()
    copy.wait_send()
    remote(src.at[core], out.at[1 - core], send_sem, recv_sem, pair).wait_recv()


def pair_swap(values, collective_id):
    return pl.pallas_call(
        pair_kernel,
        out_shape=jax.ShapeDtypeStruct(values.shape, values.dtype),
        in_specs=[VMEM],
        out_specs=VMEM,
        scratch_shapes=[pltpu.SemaphoreType.DMA] * 3,
        compiler_params=pltpu.CompilerParams(collective_id=collective_id, has_side_effects=True),
    )(values)


def relay_kernel(count, *refs):
    src, out, send_sem, recv_sem, own_sem = refs
    me = lax.axis_index("gx")
    y_chips = count // X_CHIPS
    y, x = me // X_CHIPS, lax.rem(me, X_CHIPS)

    def at(row, column):
        return lax.rem(row + y_chips, y_chips) * X_CHIPS + lax.rem(column, X_CHIPS)

    above, below = at(y + 1, x), at(y - 1, x)
    right, left = at(y, x + 1), at(y, x + 3)
    greet([{"gx": other} for other in (above, below, right, left)])
    sent = []

    def send(block, source, target):
        copy = remote(
            source, out.at[block], send_sem.at[len(sent)], recv_sem.at[block], {"gx": target}
        )
        copy.start()
        sent.append(copy)

    def arrived(block):
        remote(
            src, out.at[block], send_sem.at[0], recv_sem.at[block], {"gx": above}
        ).wait_recv()

    def across(k):
        near, far = (x + 3, right) if k % 2 == 0 else (x + 1, left)
        block = at(y + k, near)
        arrived(block)
        send(block, out.at[block], far)

    send(me, src, above)
    send(me, src, below)
    send(me, src, right)
    send(me, src, left)
    own = pltpu.make_async_copy(src, out.at[me], own_sem)
    own.start()
    half = y_chips // 2
    order = [0]
    for step in range(1, half + 1):
        order.append(y_chips - step)
        if step < half:
            order.append(step)
    for i, k in enumerate(order):
        if k:
            block = at(y + k, x)
            arrived(block)
            if half < k:
                send(block, out.at[block], above)
            elif k < half - 1:
                send(block, out.at[block], below)
            send(block, out.at[block], right)
            send(block, out.at[block], left)
        if i >= 1:
            across(order[i - 1])
    across(order[-1])
    for k in order:
        arrived(at(y + k, x + (1 if k % 2 == 0 else 3)))
        arrived(at(y + k, x + 2))
    own.wait()
    for copy in sent:
        copy.wait_send()


def relay_gather(values, collective_id):
    count = lax.axis_size("gx")
    return pl.pallas_call(
        functools.partial(relay_kernel, count),
        out_shape=jax.ShapeDtypeStruct((count,) + values.shape, values.dtype),
        in_specs=[VMEM],
        out_specs=VMEM,
        scratch_shapes=[
            pltpu.SemaphoreType.DMA((count,)),
            pltpu.SemaphoreType.DMA((count,)),
            pltpu.SemaphoreType.DMA,
        ],
        compiler_params=pltpu.CompilerParams(collective_id=collective_id, has_side_effects=True),
        cost_estimate=pl.CostEstimate(
            flops=0, bytes_accessed=40_000_000, transcendentals=0
        ),
    )(values)


def shards(
    hidden_in, norm_gain, router_weight, routes, w_gate_up, w_down, final_gain, head_weight, targets
):
    tok_rows = hidden_in.shape[0]
    width = hidden_in.shape[1]
    group_count = lax.axis_size("gx")
    lane_count = lax.axis_size("gy")
    group_index = lax.axis_index("gx")
    lane_index = lax.axis_index("gy")
    expert_count = router_weight.shape[1]
    slot_count = tok_rows // 8
    half_slots = slot_count // 2
    share_rows = tok_rows // lane_count
    columns = head_weight.shape[1]
    head_full = lax.all_gather(head_weight, "gy", axis=0, tiled=True)
    normed = rms_scale(hidden_in, norm_gain).astype(jnp.bfloat16)
    scores = jnp.dot(normed, router_weight, preferred_element_type=jnp.float32)
    chosen = routes[:, :, None] == jnp.arange(expert_count, dtype=jnp.int32)[None, None, :]
    picked = jnp.sum(jnp.where(chosen, scores[:, None, :], 0.0), -1)
    gate_values = jax.nn.softmax(picked, axis=-1).astype(jnp.bfloat16)
    gate_table = jnp.sum(jnp.where(chosen, gate_values.astype(jnp.float32)[:, :, None], 0.0), 1)
    member = jnp.sum(chosen.astype(jnp.int32), 1)
    slot_rank = jnp.cumsum(member, 0) - member
    slot_hit = (member[:, :, None] == 1) & (
        slot_rank[:, :, None] == jnp.arange(slot_count, dtype=jnp.int32)[None, None, :]
    )
    owner_expert = (
        jnp.arange(group_count, dtype=jnp.int32) * lane_count + lane_index
    ) // SPLITS
    pick_expert = (
        owner_expert[:, None] == jnp.arange(expert_count, dtype=jnp.int32)[None, :]
    ).astype(jnp.bfloat16)
    dispatch = jnp.einsum(
        "te,nec->tcn",
        pick_expert,
        slot_hit.astype(jnp.bfloat16),
        preferred_element_type=jnp.float32,
    ).astype(jnp.bfloat16)
    core = lax.rem(lane_index, 2)
    own_slots = lax.dynamic_slice_in_dim(dispatch, core * half_slots, half_slots, 1)
    outgoing = jnp.einsum(
        "tcn,nd->tcd", own_slots, normed, preferred_element_type=jnp.float32
    ).astype(jnp.bfloat16)
    expert_gate = jnp.einsum(
        "te,ne->tn",
        pick_expert,
        gate_table.astype(jnp.bfloat16),
        preferred_element_type=jnp.float32,
    )
    combine = (dispatch.astype(jnp.float32) * expert_gate[:, None, :]).astype(jnp.bfloat16)
    returned = through_experts(outgoing, w_gate_up[0], w_down[0], 1)
    partial_value = jnp.einsum(
        "tcn,tcd->nd",
        combine,
        returned.reshape(group_count, slot_count, width // 2),
        preferred_element_type=jnp.float32,
    ).astype(jnp.bfloat16)
    chips = lane_count // 2
    pieces = exchange(partial_value.reshape(chips, 2 * share_rows, width // 2), "gy", 3)
    halves = pair_swap(
        jnp.sum(pieces.astype(jnp.float32), 0).reshape(2, share_rows, width // 2), 6
    )
    summed = jnp.concatenate([halves[0], halves[1]], axis=-1)
    residual = lax.dynamic_slice_in_dim(hidden_in, lane_index * share_rows, share_rows, 0)
    layer_out = (residual.astype(jnp.float32) + summed).astype(jnp.bfloat16)
    final_states = rms_scale(layer_out, final_gain).astype(jnp.bfloat16)
    gathered = relay_gather(final_states, 4).reshape(group_count * share_rows, width)
    target_grid = targets.reshape(group_count, tok_rows)
    logits = jnp.dot(gathered, head_full, preferred_element_type=jnp.float32)
    offset = group_index * columns
    own_targets = lax.dynamic_slice_in_dim(
        target_grid, lane_index * share_rows, share_rows, 1
    ).reshape(group_count * share_rows)
    target_hits = (offset + jnp.arange(columns, dtype=jnp.int32))[None, :] == own_targets[:, None]
    local_peak = jnp.max(logits, -1)
    shifted = logits - local_peak[:, None]
    weights = jnp.exp(shifted)
    local = jnp.stack(
        [
            local_peak,
            jnp.sum(weights, -1),
            jnp.sum(weights * shifted, -1),
            jnp.sum(jnp.where(target_hits, logits, 0.0), -1),
        ]
    )
    stats = exchange(local, "gx", 5, same=True)
    peaks, masses, spreads = stats[:, 0], stats[:, 1], stats[:, 2]
    peak_value = jnp.max(peaks, 0)
    below = peaks - peak_value[None, :]
    scale = jnp.exp(below)
    total_mass = jnp.sum(masses * scale, 0)
    spread = jnp.sum(scale * (spreads + below * masses), 0)
    log_mass = jnp.log(total_mass)
    logprob = jnp.sum(stats[:, 3], 0) - peak_value - log_mass
    entropy = log_mass - spread / total_mass
    return (logprob.reshape(group_count, share_rows), entropy.reshape(group_count, share_rows))


def solution(mesh):
    return jax.shard_map(
        shards,
        mesh=mesh,
        in_specs=(
            P("gx", None),
            P(),
            P(),
            P("gx", None),
            P(("gx", "gy"), None, None),
            P(("gx", "gy"), None, None),
            P(),
            P("gy", "gx"),
            P(),
        ),
        out_specs=(P(None, "gy"), P(None, "gy")),
        check_vma=False,
    )
```
